128 devices in a mesh: row: 16 (over y, x), col: 8 (over z, core).
Axes of the slice: x: 4, y: 4, z: 4, core: 2. Of those that a mesh axis runs over, the one named last changes fastest.
Arguments:
- tokens: bfloat16 [16384, 1280], P(('row', 'col')), may hold values from -6 to 6
- image_sizes: int32 [16, 8], replicated, may hold values from 1 to 48, 256 in all within a row
- slot_of: int32 [128], replicated, may hold values from 0 to 127, as said below
- ln_gain: float32 [1, 2, 1280], replicated, may hold values from 0.25 to 1.75
- ln_bias: float32 [1, 2, 1280], replicated, may hold values from -3 to 3
- w_qkv: bfloat16 [1, 1280, 3840], P(None, 'row', 'col')
- w_out: bfloat16 [1, 1280, 1280], P(None, 'col', 'row'), may hold values from -0.15625 to 0.15625
- w_up: bfloat16 [1, 1280, 5120], P(None, 'row', 'col'), may hold values from -0.15625 to 0.15625
- w_down: bfloat16 [1, 5120, 1280], P(None, 'col', 'row'), may hold values from -0.078125 to 0.078125
- merge_gain: float32 [1280], replicated, may hold values from 0.25 to 1.75
- merge_bias: float32 [1280], replicated, may hold values from -3 to 3
- w_merge: bfloat16 [5120, 4096], P('row', 'col'), may hold values from -0.078125 to 0.078125
Outputs:
- merged_out: bfloat16 [6144, 4096], P('row', 'col')
- req_norm: float32 [128], P('row')
- req_max: float32 [128], P('row')
The draws below stay inside these ranges and needn't reach their ends.
Inputs may be any that keep to these rules, and one draw needn't show every extreme that they name: Each row of image_sizes sums to 256 and holds 48 at least once. A permutation of the slots. Request g * 8 + j goes to the row group slot_of // 8, which holds 8 slots. No row group sends more than one request to any row group.
All inputs are finite; a program needn't handle non-finite values.
Results may differ from the reference program's by a relative error of at most 0.018.
The reference program's roundings to bfloat16 on the way count: a program that leaves them out, or rounds other values in their place, can miss the bound.
Values may be sent and summed in bfloat16 or wider, within the bound.
A program may use at most 64 MiB of HBM per device.

```python
import math
import jax
import jax.numpy as jnp
import numpy as np
from jax import lax

D = 1280
HEADS = 16
HEAD_DIM = 80
FF = 5120
OUT = 4096
LAYERS = 1
IMG_ROW = 8
TOKENS = 16384
MERGED_ROW = 256
MOST = 48
N_ROW = 16
N_COL = 8


def draw_w_qkv(key, part):
    base = jax.random.normal(key, (LAYERS, D, HEADS, 3, HEAD_DIM), jnp.float32)
    base = jnp.clip(base, -6.0, 6.0) * D ** (-0.5)
    return base.reshape(LAYERS, D, 3 * HEADS * HEAD_DIM).astype(jnp.bfloat16)


def draw_slot_of(key, part):
    offsets = jax.random.permutation(jax.random.fold_in(key, 11), N_ROW)[:IMG_ROW].astype(jnp.int32)
    groups = jnp.arange(N_ROW, dtype=jnp.int32)[:, None]
    owners = (groups + offsets[None, :]) % N_ROW
    order_key = jax.random.fold_in(key, 13)
    orders = jax.vmap(lambda index: jax.random.permutation(jax.random.fold_in(order_key, index), IMG_ROW))(jnp.arange(N_ROW, dtype=jnp.int32))
    columns = jnp.arange(IMG_ROW, dtype=jnp.int32)[None, :]
    slots = owners * IMG_ROW + orders[owners, columns].astype(jnp.int32)
    return slots.reshape(-1).astype(jnp.int32)


def levels(key, dims, shards, low, largest):
    factor_of = 1.0
    for axis_at, blocks in shards:
        heights = jax.random.uniform(jax.random.fold_in(jax.random.fold_in(key, 6), axis_at), (blocks,), jnp.float32, low / len(shards), largest / len(shards))
        factor_of = factor_of * jnp.repeat(jnp.exp(heights), dims[axis_at] // blocks).reshape((-1,) + (1,) * (len(dims) - 1 - axis_at))
    return factor_of


def split_up(amount, total, limit, slope):
    loads = [(1 << 20) // math.isqrt(grade ** slope) + 1 for grade in range(2, amount + 1)]
    surplus, given = total - limit - (amount - 1), [1] * (amount - 1)
    while surplus > 0:
        free = [i for i in range(amount - 1) if given[i] < limit]
        pool, remaining = sum([loads[i] for i in free]), surplus
        for i in free:
            addition = min(limit - given[i], max(1, remaining * loads[i] // pool), surplus)
            given[i] = given[i] + addition
            surplus = surplus - addition
    return np.array([limit] + given)


def ragged(key, amount, total, limit, lean):
    if amount == 2:
        one = jax.random.randint(key, (), max(1, total - limit), min(limit, total - 1) + 1)
        return jnp.stack([one, total - one])
    sizes = jnp.asarray(split_up(amount, total, limit, lean), jnp.int32)
    twos = (amount - 1) // 2
    donor, receiver = sizes[1:1 + 2 * twos:2], sizes[2:2 + 2 * twos:2]
    margin = jnp.minimum(donor - 1, limit - receiver)
    passed = jax.random.randint(jax.random.fold_in(key, 1), (twos,), 0, 1 << 20) % (margin + 1)
    sizes = sizes.at[1:1 + 2 * twos:2].set(donor - passed).at[2:2 + 2 * twos:2].set(receiver + passed)
    return sizes[jax.random.permutation(jax.random.fold_in(key, 2), amount)]


def gaussian(rng, dims, scale, reach, pieces=(), kind=jnp.bfloat16):
    factor_of = levels(rng, dims, pieces, -0.22, 0.18) if pieces else 1.0
    result = jax.random.normal(rng, dims, jnp.float32) * scale * factor_of
    return jnp.minimum(jnp.maximum(result, -reach), reach).astype(kind)


def setup_inputs(seed: int = 0) -> dict:
    seeds = jax.random.split(jax.random.key(seed), 13)
    return {
        "tokens": gaussian(seeds[0], (TOKENS, D), 1.0, 6.0, ((0, 128),)),
        "image_sizes": jax.vmap(lambda own: ragged(own, IMG_ROW, MERGED_ROW, MOST, 2))(jax.random.split(seeds[1], N_ROW)).reshape((N_ROW, IMG_ROW)).astype(jnp.int32),
        "slot_of": draw_slot_of(jax.random.fold_in(seeds[12], 71), 0),
        "ln_gain": jnp.clip(1.0 + 0.15 * jax.random.normal(seeds[3], (LAYERS, 2, D), jnp.float32), 0.25, 1.75),
        "ln_bias": gaussian(seeds[4], (LAYERS, 2, D), 0.5, 3.0, (), jnp.float32),
        "w_qkv": draw_w_qkv(jax.random.fold_in(seeds[12], 71), 0),
        "w_out": gaussian(seeds[6], (LAYERS, HEADS * HEAD_DIM, D), (HEADS * HEAD_DIM) ** -0.5, 0.15625, ((1, 8), (2, 16))),
        "w_up": gaussian(seeds[7], (LAYERS, D, FF), D ** -0.5, 0.15625, ((1, 16), (2, 8))),
        "w_down": gaussian(seeds[8], (LAYERS, FF, D), FF ** -0.5, 0.078125, ((1, 8), (2, 16))),
        "merge_gain": jnp.clip(1.0 + 0.15 * jax.random.normal(seeds[9], (D,), jnp.float32), 0.25, 1.75),
        "merge_bias": gaussian(seeds[10], (D,), 0.5, 3.0, (), jnp.float32),
        "w_merge": gaussian(seeds[11], (4 * D, OUT), (4 * D) ** -0.5, 0.078125, ((0, 16), (1, 8))),
    }


def layer_norm(values, gain, bias):
    center = lax.optimization_barrier(jnp.mean(values, axis=-1, keepdims=True))
    shifted = values - center
    spread = lax.optimization_barrier(jnp.mean(shifted * shifted, axis=-1, keepdims=True))
    return shifted * lax.rsqrt(spread + 1e-06) * gain + bias

def segment_ids(sizes_row, count):
    bounds = jnp.cumsum(sizes_row).astype(jnp.int32)
    merged_index = (jnp.arange(count, dtype=jnp.int32) // 4).astype(jnp.int32)
    return lax.optimization_barrier(jnp.sum((merged_index[:, None] >= bounds[None, :]).astype(jnp.int32), axis=1)).astype(jnp.int32)

def attend_group(qkv_group, segments):
    query = qkv_group[:, :, 0].astype(jnp.float32)
    keys = qkv_group[:, :, 1].astype(jnp.float32)
    values = qkv_group[:, :, 2].astype(jnp.float32)
    scores = jnp.einsum('qhd,khd->hqk', query, keys, precision=lax.Precision.HIGHEST) * HEAD_DIM ** (-0.5)
    same = segments[:, None] == segments[None, :]
    scores = jnp.where(same[None], scores, -1e+30)
    peak = lax.optimization_barrier(jnp.max(scores, axis=-1, keepdims=True))
    expo = jnp.exp(scores - peak)
    weights = (expo / lax.optimization_barrier(jnp.sum(expo, axis=-1, keepdims=True))).astype(jnp.bfloat16)
    context = jnp.einsum('hqk,khd->qhd', weights.astype(jnp.float32), values, precision=lax.Precision.HIGHEST)
    return context.astype(jnp.bfloat16).reshape(qkv_group.shape[0], HEADS * HEAD_DIM)

def group_sum(left, right):
    width = left.shape[1] // N_COL

    def add_group(index, accum):
        offset = (index * width).astype(jnp.int32)
        left_part = lax.dynamic_slice_in_dim(left, offset, width, 1)
        right_part = lax.dynamic_slice_in_dim(right, offset, width, 0)
        term = jnp.dot(left_part, right_part, preferred_element_type=jnp.float32)
        return accum + lax.optimization_barrier(term.astype(jnp.bfloat16)).astype(jnp.float32)
    return lax.fori_loop(0, N_COL, add_group, jnp.zeros((left.shape[0], right.shape[1]), jnp.float32))

def reference(tokens, image_sizes, slot_of, ln_gain, ln_bias, w_qkv, w_out, w_up, w_down, merge_gain, merge_bias, w_merge):
    count_all = tokens.shape[0]
    tok_row = count_all // N_ROW
    merged_row = tok_row // 4
    segments = jax.vmap(lambda sizes_row: segment_ids(sizes_row, tok_row))(image_sizes)
    stream = tokens
    for layer in range(LAYERS):
        normed = layer_norm(stream.astype(jnp.float32), ln_gain[layer, 0], ln_bias[layer, 0]).astype(jnp.bfloat16)
        qkv = jnp.dot(normed, w_qkv[layer], preferred_element_type=jnp.float32).astype(jnp.bfloat16)
        qkv = qkv.reshape(N_ROW, tok_row, HEADS, 3, HEAD_DIM)
        context = lax.map(lambda pair: attend_group(pair[0], pair[1]), (qkv, segments)).reshape(count_all, HEADS * HEAD_DIM)
        stream = (stream.astype(jnp.float32) + group_sum(context, w_out[layer])).astype(jnp.bfloat16)
        normed = layer_norm(stream.astype(jnp.float32), ln_gain[layer, 1], ln_bias[layer, 1]).astype(jnp.bfloat16)
        hidden = jax.nn.gelu(jnp.dot(normed, w_up[layer], preferred_element_type=jnp.float32), approximate=False).astype(jnp.bfloat16)
        stream = (stream.astype(jnp.float32) + group_sum(hidden, w_down[layer])).astype(jnp.bfloat16)
    merged = layer_norm(stream.astype(jnp.float32), merge_gain, merge_bias).astype(jnp.bfloat16).reshape(count_all // 4, 4 * D)
    projected = jnp.dot(merged, w_merge, preferred_element_type=jnp.float32).astype(jnp.bfloat16)
    reqs = slot_of.shape[0]
    numbers = jnp.arange(reqs, dtype=jnp.int32)
    req_at_slot = lax.optimization_barrier(jnp.sum(jnp.where(slot_of[None, :] == numbers[:, None], numbers[None, :], 0), axis=1)).astype(jnp.int32)
    starts = (jnp.cumsum(image_sizes, axis=1) - image_sizes).astype(jnp.int32).reshape(-1)
    sizes_flat = image_sizes.reshape(-1).astype(jnp.int32)
    rows_out = jnp.arange(reqs * MOST, dtype=jnp.int32)
    slot_index = rows_out // MOST
    inner = rows_out % MOST
    request = req_at_slot[slot_index]
    group = request // IMG_ROW
    source = (group * merged_row + starts[request] + inner).astype(jnp.int32)
    valid = inner < sizes_flat[request]
    taken = projected[jnp.clip(source, 0, count_all // 4 - 1)]
    placed = jnp.where(valid[:, None], taken, jnp.zeros_like(taken))
    blocks = placed.astype(jnp.float32).reshape(reqs, MOST, OUT)
    squares = lax.optimization_barrier(jnp.sum(blocks * blocks, axis=(1, 2)))
    peaks = lax.optimization_barrier(jnp.max(jnp.abs(blocks), axis=(1, 2)))
    slot_size = sizes_flat[req_at_slot].astype(jnp.float32)
    req_norm = jnp.sqrt(squares / (slot_size * OUT) + 1e-06)
    merged_out = (blocks / req_norm[:, None, None]).astype(jnp.bfloat16).reshape(reqs * MOST, OUT)
    return (merged_out, req_norm, peaks)
```

```python
import jax
import jax.numpy as jnp
from jax import lax
from jax.sharding import PartitionSpec as P

D = 1280
HEAD_DIM = 80
OUT = 4096
IMG_ROW = 8


def layer_norm(values, gain, bias):
    center = jnp.mean(values, axis=-1, keepdims=True)
    shifted = values - center
    spread = jnp.mean(shifted * shifted, axis=-1, keepdims=True)
    return shifted * lax.rsqrt(spread + 1e-06) * gain + bias


def segment_ids(sizes_row, count):
    bounds = jnp.cumsum(sizes_row)
    merged_index = jnp.arange(count, dtype=jnp.int32) // 4
    return jnp.sum((merged_index[:, None] >= bounds[None, :]).astype(jnp.int32), axis=1)


def attend(qkv, segments):
    count = qkv.shape[0]
    width = min(512, count)
    query = qkv[:, :, 0]
    keys = qkv[:, :, 1]
    values = qkv[:, :, 2]
    results = []
    for offset in range(0, count, width):
        scores = jnp.einsum(
            "qhd,khd->hqk", query[offset : offset + width], keys, preferred_element_type=jnp.float32
        ) * HEAD_DIM ** (-0.5)
        same = segments[offset : offset + width, None] == segments[None, :]
        scores = jnp.where(same[None], scores, -1e30)
        peak = jnp.max(scores, axis=-1, keepdims=True)
        expo = jnp.exp(scores - peak)
        weights = (expo / jnp.sum(expo, axis=-1, keepdims=True)).astype(jnp.bfloat16)
        context = jnp.einsum("hqk,khd->qhd", weights, values, preferred_element_type=jnp.float32)
        results.append(context.astype(jnp.bfloat16).reshape(width, -1))
    return jnp.concatenate(results, axis=0)


def row_collect(flat):
    n_row = lax.axis_size("row")
    row_index = lax.axis_index("row")
    pieces = [flat]
    for shift in range(1, n_row):
        pairs = [(i, (i + shift) % n_row) for i in range(n_row)]
        pieces.append(lax.ppermute(flat, "row", pairs))
    stacked = jnp.stack(pieces[::-1])
    doubled = jnp.concatenate([stacked, stacked], axis=0)
    return lax.dynamic_slice_in_dim(doubled, (n_row - 1 - row_index) % n_row, n_row, 0)


def local(
    tokens,
    image_sizes,
    slot_of,
    ln_gain,
    ln_bias,
    w_qkv,
    w_out,
    w_up,
    w_down,
    merge_gain,
    merge_bias,
    w_merge,
):
    n_col = lax.axis_size("col")
    n_row = lax.axis_size("row")
    row_index = lax.axis_index("row")
    tok_dev = tokens.shape[0]
    tok_row = tok_dev * n_col
    merged_row = tok_row // 4
    most = merged_row * 3 // 16
    sizes_here = lax.dynamic_index_in_dim(image_sizes, row_index, 0, keepdims=False)
    segments = segment_ids(sizes_here, tok_row)

    qkv_size = w_qkv[0].size
    first = row_collect(jnp.concatenate([w_qkv[0].reshape(-1), w_out[0].reshape(-1)]))
    up_size = w_up[0].size
    second = row_collect(jnp.concatenate([w_up[0].reshape(-1), w_down[0].reshape(-1)]))
    third = row_collect(w_merge.reshape(-1))
    qkv_full = first[:, :qkv_size].reshape(n_row * w_qkv.shape[1], w_qkv.shape[2])
    out_full = (
        first[:, qkv_size:]
        .reshape(n_row, w_out.shape[1], w_out.shape[2])
        .transpose(1, 0, 2)
        .reshape(w_out.shape[1], n_row * w_out.shape[2])
    )
    up_full = second[:, :up_size].reshape(n_row * w_up.shape[1], w_up.shape[2])
    down_full = (
        second[:, up_size:]
        .reshape(n_row, w_down.shape[1], w_down.shape[2])
        .transpose(1, 0, 2)
        .reshape(w_down.shape[1], n_row * w_down.shape[2])
    )
    merge_full = third.reshape(n_row * w_merge.shape[0], w_merge.shape[1])

    stream = tokens
    normed = layer_norm(stream.astype(jnp.float32), ln_gain[0, 0], ln_bias[0, 0]).astype(
        jnp.bfloat16
    )
    normed_all = lax.all_gather(normed, "col", axis=0, tiled=True)
    qkv = jnp.dot(normed_all, qkv_full, preferred_element_type=jnp.float32)
    qkv = qkv.astype(jnp.bfloat16).reshape(tok_row, -1, 3, HEAD_DIM)
    context = attend(qkv, segments)
    attn_terms = jnp.dot(context, out_full, preferred_element_type=jnp.float32)
    attn_out = lax.psum_scatter(
        attn_terms.astype(jnp.bfloat16), "col", scatter_dimension=0, tiled=True
    ).astype(jnp.float32)
    stream = (stream.astype(jnp.float32) + attn_out).astype(jnp.bfloat16)
    normed = layer_norm(stream.astype(jnp.float32), ln_gain[0, 1], ln_bias[0, 1]).astype(
        jnp.bfloat16
    )
    normed_mlp = lax.all_gather(normed, "col", axis=0, tiled=True)
    up_value = jnp.dot(normed_mlp, up_full, preferred_element_type=jnp.float32)
    hidden = jax.nn.gelu(up_value, approximate=False).astype(jnp.bfloat16)
    mlp_terms = jnp.dot(hidden, down_full, preferred_element_type=jnp.float32)
    mlp_out = lax.psum_scatter(
        mlp_terms.astype(jnp.bfloat16), "col", scatter_dimension=0, tiled=True
    ).astype(jnp.float32)
    stream = (stream.astype(jnp.float32) + mlp_out).astype(jnp.bfloat16)
    merged = layer_norm(stream.astype(jnp.float32), merge_gain, merge_bias).astype(jnp.bfloat16)
    merged = merged.reshape(tok_dev // 4, 4 * D)
    merged_all = lax.all_gather(merged, "col", axis=0, tiled=True)
    out_dev = w_merge.shape[1]
    projected = jnp.dot(merged_all, merge_full, preferred_element_type=jnp.float32).astype(
        jnp.bfloat16
    )

    reqs = slot_of.shape[0]
    numbers = jnp.arange(reqs, dtype=jnp.int32)
    req_at_slot = jnp.sum(
        jnp.where(slot_of[None, :] == numbers[:, None], numbers[None, :], 0), axis=1
    )
    starts = jnp.cumsum(image_sizes, axis=1) - image_sizes
    sizes_flat = image_sizes.reshape(-1)
    inner = jnp.arange(most, dtype=jnp.int32)
    groups = jnp.arange(n_row, dtype=jnp.int32)
    my_dest = lax.dynamic_slice_in_dim(slot_of, row_index * IMG_ROW, IMG_ROW) // IMG_ROW
    my_starts = lax.dynamic_index_in_dim(starts, row_index, 0, keepdims=False)
    match = my_dest[None, :] == groups[:, None]
    start_to = jnp.sum(jnp.where(match, my_starts[None, :], 0), axis=1)
    padded = jnp.concatenate([projected, jnp.zeros((most, out_dev), projected.dtype)], axis=0)
    rows = jnp.clip(start_to[:, None] + inner[None, :], 0, padded.shape[0] - 1)
    send = jnp.take(padded, rows.reshape(-1), axis=0).reshape(n_row, most, out_dev)
    recv = lax.all_to_all(send, "row", 0, 0, tiled=True)

    request = lax.dynamic_slice_in_dim(req_at_slot, row_index * IMG_ROW, IMG_ROW)
    source = request // IMG_ROW
    taken = jnp.take(recv, source, axis=0)
    valid = inner[None, :] < sizes_flat[request][:, None]
    blocks = jnp.where(valid[:, :, None], taken, jnp.zeros_like(taken)).astype(jnp.float32)
    squares = jnp.sum(blocks * blocks, axis=(1, 2))
    peaks = jnp.max(jnp.abs(blocks), axis=(1, 2))
    stats = lax.all_gather(jnp.concatenate([squares, peaks]), "col", axis=0, tiled=False)
    squares = jnp.sum(stats[:, :IMG_ROW], axis=0)
    peaks = jnp.max(stats[:, IMG_ROW:], axis=0)
    slot_size = sizes_flat[request].astype(jnp.float32)
    req_norm = jnp.sqrt(squares / (slot_size * OUT) + 1e-06)
    merged_out = (
        (blocks / req_norm[:, None, None]).astype(jnp.bfloat16).reshape(IMG_ROW * most, out_dev)
    )
    return (merged_out, req_norm, peaks)


def solution(mesh):
    in_specs = (
        P(("row", "col"), None),
        P(),
        P(),
        P(),
        P(),
        P(None, "row", "col"),
        P(None, "col", "row"),
        P(None, "row", "col"),
        P(None, "col", "row"),
        P(),
        P(),
        P("row", "col"),
    )
    out_specs = (P("row", "col"), P("row"), P("row"))
    return jax.shard_map(local, mesh=mesh, in_specs=in_specs, out_specs=out_specs, check_vma=False)
```

```python
import jax
import jax.numpy as jnp
from jax import lax
from jax.sharding import PartitionSpec as P

D = 1280
HEAD_DIM = 80
OUT = 4096
IMG_ROW = 8


def layer_norm(values, gain, bias):
    center = jnp.mean(values, axis=-1, keepdims=True)
    shifted = values - center
    spread = jnp.mean(shifted * shifted, axis=-1, keepdims=True)
    return shifted * lax.rsqrt(spread + 1e-06) * gain + bias


def segment_ids(sizes_row, count):
    bounds = jnp.cumsum(sizes_row)
    merged_index = jnp.arange(count, dtype=jnp.int32) // 4
    return jnp.sum((merged_index[:, None] >= bounds[None, :]).astype(jnp.int32), axis=1)


def attend(qkv, segments):
    count = qkv.shape[0]
    width = min(512, count)
    query = qkv[:, :, 0]
    keys = qkv[:, :, 1]
    values = qkv[:, :, 2]
    results = []
    for offset in range(0, count, width):
        scores = jnp.einsum(
            "qhd,khd->hqk", query[offset : offset + width], keys, preferred_element_type=jnp.float32
        ) * HEAD_DIM ** (-0.5)
        same = segments[offset : offset + width, None] == segments[None, :]
        scores = jnp.where(same[None], scores, -1e30)
        peak = jnp.max(scores, axis=-1, keepdims=True)
        expo = jnp.exp(scores - peak)
        weights = (expo / jnp.sum(expo, axis=-1, keepdims=True)).astype(jnp.bfloat16)
        context = jnp.einsum("hqk,khd->qhd", weights, values, preferred_element_type=jnp.float32)
        results.append(context.astype(jnp.bfloat16).reshape(width, -1))
    return jnp.concatenate(results, axis=0)


def row_gather(block):
    n_row = lax.axis_size("row")
    send = jnp.broadcast_to(block[None], (n_row,) + block.shape)
    received = lax.all_to_all(send, "row", 0, 0, tiled=True)
    return received.reshape((n_row * block.shape[0],) + block.shape[1:])


def local(
    tokens,
    image_sizes,
    slot_of,
    ln_gain,
    ln_bias,
    w_qkv,
    w_out,
    w_up,
    w_down,
    merge_gain,
    merge_bias,
    w_merge,
):
    n_col = lax.axis_size("col")
    n_row = lax.axis_size("row")
    row_index = lax.axis_index("row")
    tok_dev = tokens.shape[0]
    tok_row = tok_dev * n_col
    merged_row = tok_row // 4
    most = merged_row * 3 // 16
    sizes_here = lax.dynamic_index_in_dim(image_sizes, row_index, 0, keepdims=False)
    segments = segment_ids(sizes_here, tok_row)

    qkv_cols = w_qkv.shape[2]
    first = row_gather(jnp.concatenate([w_qkv[0], w_out[0].T], axis=1))
    up_cols = w_up.shape[2]
    second = row_gather(jnp.concatenate([w_up[0], w_down[0].T], axis=1))
    merge_full = row_gather(w_merge)
    qkv_full = first[:, :qkv_cols]
    out_t = first[:, qkv_cols:]
    up_full = second[:, :up_cols]
    down_t = second[:, up_cols:]
    contract_t = (((1,), (1,)), ((), ()))

    stream = tokens
    normed = layer_norm(stream.astype(jnp.float32), ln_gain[0, 0], ln_bias[0, 0]).astype(
        jnp.bfloat16
    )
    normed_all = lax.all_gather(normed, "col", axis=0, tiled=True)
    qkv = jnp.dot(normed_all, qkv_full, preferred_element_type=jnp.float32)
    qkv = qkv.astype(jnp.bfloat16).reshape(tok_row, -1, 3, HEAD_DIM)
    context = attend(qkv, segments)
    attn_terms = lax.dot_general(
        context, out_t, contract_t, preferred_element_type=jnp.float32
    )
    attn_out = lax.psum_scatter(
        attn_terms.astype(jnp.bfloat16), "col", scatter_dimension=0, tiled=True
    ).astype(jnp.float32)
    stream = (stream.astype(jnp.float32) + attn_out).astype(jnp.bfloat16)
    normed = layer_norm(stream.astype(jnp.float32), ln_gain[0, 1], ln_bias[0, 1]).astype(
        jnp.bfloat16
    )
    normed_mlp = lax.all_gather(normed, "col", axis=0, tiled=True)
    up_value = jnp.dot(normed_mlp, up_full, preferred_element_type=jnp.float32)
    hidden = jax.nn.gelu(up_value, approximate=False).astype(jnp.bfloat16)
    mlp_terms = lax.dot_general(
        hidden, down_t, contract_t, preferred_element_type=jnp.float32
    )
    mlp_out = lax.psum_scatter(
        mlp_terms.astype(jnp.bfloat16), "col", scatter_dimension=0, tiled=True
    ).astype(jnp.float32)
    stream = (stream.astype(jnp.float32) + mlp_out).astype(jnp.bfloat16)
    merged = layer_norm(stream.astype(jnp.float32), merge_gain, merge_bias).astype(jnp.bfloat16)
    merged = merged.reshape(tok_dev // 4, 4 * D)
    merged_all = lax.all_gather(merged, "col", axis=0, tiled=True)
    out_dev = w_merge.shape[1]
    projected = jnp.dot(merged_all, merge_full, preferred_element_type=jnp.float32).astype(
        jnp.bfloat16
    )

    reqs = slot_of.shape[0]
    numbers = jnp.arange(reqs, dtype=jnp.int32)
    req_at_slot = jnp.sum(
        jnp.where(slot_of[None, :] == numbers[:, None], numbers[None, :], 0), axis=1
    )
    starts = jnp.cumsum(image_sizes, axis=1) - image_sizes
    sizes_flat = image_sizes.reshape(-1)
    inner = jnp.arange(most, dtype=jnp.int32)
    groups = jnp.arange(n_row, dtype=jnp.int32)
    my_dest = lax.dynamic_slice_in_dim(slot_of, row_index * IMG_ROW, IMG_ROW) // IMG_ROW
    my_starts = lax.dynamic_index_in_dim(starts, row_index, 0, keepdims=False)
    match = my_dest[None, :] == groups[:, None]
    start_to = jnp.sum(jnp.where(match, my_starts[None, :], 0), axis=1)
    padded = jnp.concatenate([projected, jnp.zeros((most, out_dev), projected.dtype)], axis=0)
    rows = jnp.clip(start_to[:, None] + inner[None, :], 0, padded.shape[0] - 1)
    send = jnp.take(padded, rows.reshape(-1), axis=0).reshape(n_row, most, out_dev)
    recv = lax.all_to_all(send, "row", 0, 0, tiled=True)

    request = lax.dynamic_slice_in_dim(req_at_slot, row_index * IMG_ROW, IMG_ROW)
    source = request // IMG_ROW
    taken = jnp.take(recv, source, axis=0)
    valid = inner[None, :] < sizes_flat[request][:, None]
    blocks = jnp.where(valid[:, :, None], taken, jnp.zeros_like(taken)).astype(jnp.float32)
    squares = jnp.sum(blocks * blocks, axis=(1, 2))
    peaks = jnp.max(jnp.abs(blocks), axis=(1, 2))
    stats = lax.all_gather(jnp.concatenate([squares, peaks]), "col", axis=0, tiled=False)
    squares = jnp.sum(stats[:, :IMG_ROW], axis=0)
    peaks = jnp.max(stats[:, IMG_ROW:], axis=0)
    slot_size = sizes_flat[request].astype(jnp.float32)
    req_norm = jnp.sqrt(squares / (slot_size * OUT) + 1e-06)
    merged_out = (
        (blocks / req_norm[:, None, None]).astype(jnp.bfloat16).reshape(IMG_ROW * most, out_dev)
    )
    return (merged_out, req_norm, peaks)


def solution(mesh):
    in_specs = (
        P(("row", "col"), None),
        P(),
        P(),
        P(),
        P(),
        P(None, "row", "col"),
        P(None, "col", "row"),
        P(None, "row", "col"),
        P(None, "col", "row"),
        P(),
        P(),
        P("row", "col"),
    )
    out_specs = (P("row", "col"), P("row"), P("row"))
    return jax.shard_map(local, mesh=mesh, in_specs=in_specs, out_specs=out_specs, check_vma=False)
```

```python
import jax
import jax.numpy as jnp
from jax import lax
from jax.sharding import PartitionSpec as P

D = 1280
HEAD_DIM = 80
OUT = 4096
IMG_ROW = 8


def layer_norm(values, gain, bias):
    center = jnp.mean(values, axis=-1, keepdims=True)
    shifted = values - center
    spread = jnp.mean(shifted * shifted, axis=-1, keepdims=True)
    return shifted * lax.rsqrt(spread + 1e-06) * gain + bias


def segment_ids(sizes_row, count):
    bounds = jnp.cumsum(sizes_row)
    merged_index = jnp.arange(count, dtype=jnp.int32) // 4
    return jnp.sum((merged_index[:, None] >= bounds[None, :]).astype(jnp.int32), axis=1)


def attend(qkv, segments):
    count = qkv.shape[0]
    width = min(512, count)
    query = qkv[:, :, 0]
    keys = qkv[:, :, 1]
    values = qkv[:, :, 2]
    results = []
    for offset in range(0, count, width):
        scores = jnp.einsum(
            "qhd,khd->hqk", query[offset : offset + width], keys, preferred_element_type=jnp.float32
        ) * HEAD_DIM ** (-0.5)
        same = segments[offset : offset + width, None] == segments[None, :]
        scores = jnp.where(same[None], scores, -1e30)
        peak = jnp.max(scores, axis=-1, keepdims=True)
        expo = jnp.exp(scores - peak)
        weights = (expo / jnp.sum(expo, axis=-1, keepdims=True)).astype(jnp.bfloat16)
        context = jnp.einsum("hqk,khd->qhd", weights, values, preferred_element_type=jnp.float32)
        results.append(context.astype(jnp.bfloat16).reshape(width, -1))
    return jnp.concatenate(results, axis=0)


def row_gather(block):
    n_row = lax.axis_size("row")
    send = jnp.broadcast_to(block[None], (n_row,) + block.shape)
    received = lax.all_to_all(send, "row", 0, 0, tiled=True)
    return received.reshape((n_row * block.shape[0],) + block.shape[1:])


def local(
    tokens,
    image_sizes,
    slot_of,
    ln_gain,
    ln_bias,
    w_qkv,
    w_out,
    w_up,
    w_down,
    merge_gain,
    merge_bias,
    w_merge,
):
    n_col = lax.axis_size("col")
    n_row = lax.axis_size("row")
    row_index = lax.axis_index("row")
    tok_dev = tokens.shape[0]
    tok_row = tok_dev * n_col
    merged_row = tok_row // 4
    most = merged_row * 3 // 16
    sizes_here = lax.dynamic_index_in_dim(image_sizes, row_index, 0, keepdims=False)
    segments = segment_ids(sizes_here, tok_row)

    qkv_cols = w_qkv.shape[2]
    first = row_gather(jnp.concatenate([w_qkv[0], w_out[0].T], axis=1))
    up_cols = w_up.shape[2]
    down_cols = w_down.shape[1]
    rest = w_merge.reshape(w_up.shape[1], -1)
    second = row_gather(jnp.concatenate([w_up[0], w_down[0].T, rest], axis=1))
    qkv_full = first[:, :qkv_cols]
    out_t = first[:, qkv_cols:]
    up_full = second[:, :up_cols]
    down_t = second[:, up_cols : up_cols + down_cols]
    merge_full = second[:, up_cols + down_cols :].reshape(-1, w_merge.shape[1])
    contract_t = (((1,), (1,)), ((), ()))

    stream = tokens
    normed = layer_norm(stream.astype(jnp.float32), ln_gain[0, 0], ln_bias[0, 0]).astype(
        jnp.bfloat16
    )
    normed_all = lax.all_gather(normed, "col", axis=0, tiled=True)
    qkv = jnp.dot(normed_all, qkv_full, preferred_element_type=jnp.float32)
    qkv = qkv.astype(jnp.bfloat16).reshape(tok_row, -1, 3, HEAD_DIM)
    context = attend(qkv, segments)
    attn_terms = lax.dot_general(
        context, out_t, contract_t, preferred_element_type=jnp.float32
    )
    attn_out = lax.psum_scatter(
        attn_terms.astype(jnp.bfloat16), "col", scatter_dimension=0, tiled=True
    ).astype(jnp.float32)
    stream = (stream.astype(jnp.float32) + attn_out).astype(jnp.bfloat16)
    normed = layer_norm(stream.astype(jnp.float32), ln_gain[0, 1], ln_bias[0, 1]).astype(
        jnp.bfloat16
    )
    normed_mlp = lax.all_gather(normed, "col", axis=0, tiled=True)
    up_value = jnp.dot(normed_mlp, up_full, preferred_element_type=jnp.float32)
    hidden = jax.nn.gelu(up_value, approximate=False).astype(jnp.bfloat16)
    mlp_terms = lax.dot_general(
        hidden, down_t, contract_t, preferred_element_type=jnp.float32
    )
    mlp_out = lax.psum_scatter(
        mlp_terms.astype(jnp.bfloat16), "col", scatter_dimension=0, tiled=True
    ).astype(jnp.float32)
    stream = (stream.astype(jnp.float32) + mlp_out).astype(jnp.bfloat16)
    merged = layer_norm(stream.astype(jnp.float32), merge_gain, merge_bias).astype(jnp.bfloat16)
    merged = merged.reshape(tok_dev // 4, 4 * D)
    merged_all = lax.all_gather(merged, "col", axis=0, tiled=True)
    out_dev = w_merge.shape[1]
    projected = jnp.dot(merged_all, merge_full, preferred_element_type=jnp.float32).astype(
        jnp.bfloat16
    )

    reqs = slot_of.shape[0]
    numbers = jnp.arange(reqs, dtype=jnp.int32)
    req_at_slot = jnp.sum(
        jnp.where(slot_of[None, :] == numbers[:, None], numbers[None, :], 0), axis=1
    )
    starts = jnp.cumsum(image_sizes, axis=1) - image_sizes
    sizes_flat = image_sizes.reshape(-1)
    inner = jnp.arange(most, dtype=jnp.int32)
    groups = jnp.arange(n_row, dtype=jnp.int32)
    my_dest = lax.dynamic_slice_in_dim(slot_of, row_index * IMG_ROW, IMG_ROW) // IMG_ROW
    my_starts = lax.dynamic_index_in_dim(starts, row_index, 0, keepdims=False)
    match = my_dest[None, :] == groups[:, None]
    start_to = jnp.sum(jnp.where(match, my_starts[None, :], 0), axis=1)
    padded = jnp.concatenate([projected, jnp.zeros((most, out_dev), projected.dtype)], axis=0)
    rows = jnp.clip(start_to[:, None] + inner[None, :], 0, padded.shape[0] - 1)
    send = jnp.take(padded, rows.reshape(-1), axis=0).reshape(n_row, most, out_dev)
    recv = lax.all_to_all(send, "row", 0, 0, tiled=True)

    owner = segment_ids(sizes_here, merged_row * 4)[::4]
    own = owner[:, None] == jnp.arange(IMG_ROW, dtype=jnp.int32)[None, :]
    proj32 = projected.astype(jnp.float32)
    row_sq = jnp.sum(proj32 * proj32, axis=1)
    row_peak = jnp.max(jnp.abs(proj32), axis=1)
    part_sq = jnp.sum(jnp.where(own, row_sq[:, None], 0.0), axis=0)
    part_peak = jnp.max(jnp.where(own, row_peak[:, None], 0.0), axis=0)
    stats = lax.all_gather(
        jnp.concatenate([part_sq, part_peak]), ("row", "col"), axis=0, tiled=False
    ).reshape(n_row, n_col, 2, IMG_ROW)
    req_sq = jnp.sum(stats[:, :, 0], axis=1).reshape(-1)
    req_peak = jnp.max(stats[:, :, 1], axis=1).reshape(-1)

    request = lax.dynamic_slice_in_dim(req_at_slot, row_index * IMG_ROW, IMG_ROW)
    source = request // IMG_ROW
    taken = jnp.take(recv, source, axis=0)
    valid = inner[None, :] < sizes_flat[request][:, None]
    blocks = jnp.where(valid[:, :, None], taken, jnp.zeros_like(taken)).astype(jnp.float32)
    squares = req_sq[request]
    peaks = req_peak[request]
    slot_size = sizes_flat[request].astype(jnp.float32)
    req_norm = jnp.sqrt(squares / (slot_size * OUT) + 1e-06)
    merged_out = (
        (blocks / req_norm[:, None, None]).astype(jnp.bfloat16).reshape(IMG_ROW * most, out_dev)
    )
    return (merged_out, req_norm, peaks)


def solution(mesh):
    in_specs = (
        P(("row", "col"), None),
        P(),
        P(),
        P(),
        P(),
        P(None, "row", "col"),
        P(None, "col", "row"),
        P(None, "row", "col"),
        P(None, "col", "row"),
        P(),
        P(),
        P("row", "col"),
    )
    out_specs = (P("row", "col"), P("row"), P("row"))
    return jax.shard_map(local, mesh=mesh, in_specs=in_specs, out_specs=out_specs, check_vma=False)
```

```python
import jax
import jax.numpy as jnp
from jax import lax
from jax.sharding import PartitionSpec as P

D = 1280
HEAD_DIM = 80
OUT = 4096
IMG_ROW = 8


def layer_norm(values, gain, bias):
    center = jnp.mean(values, axis=-1, keepdims=True)
    shifted = values - center
    spread = jnp.mean(shifted * shifted, axis=-1, keepdims=True)
    return shifted * lax.rsqrt(spread + 1e-06) * gain + bias


def segment_ids(sizes_row, count):
    bounds = jnp.cumsum(sizes_row)
    merged_index = jnp.arange(count, dtype=jnp.int32) // 4
    return jnp.sum((merged_index[:, None] >= bounds[None, :]).astype(jnp.int32), axis=1)


def attend(qkv, segments):
    count = qkv.shape[0]
    width = min(512, count)
    query = qkv[:, :, 0]
    keys = qkv[:, :, 1]
    values = qkv[:, :, 2]
    results = []
    for offset in range(0, count, width):
        scores = jnp.einsum(
            "qhd,khd->hqk", query[offset : offset + width], keys, preferred_element_type=jnp.float32
        ) * HEAD_DIM ** (-0.5)
        same = segments[offset : offset + width, None] == segments[None, :]
        scores = jnp.where(same[None], scores, -1e30)
        peak = jnp.max(scores, axis=-1, keepdims=True)
        expo = jnp.exp(scores - peak)
        weights = (expo / jnp.sum(expo, axis=-1, keepdims=True)).astype(jnp.bfloat16)
        context = jnp.einsum("hqk,khd->qhd", weights, values, preferred_element_type=jnp.float32)
        results.append(context.astype(jnp.bfloat16).reshape(width, -1))
    return jnp.concatenate(results, axis=0)


def row_gather(block):
    n_row = lax.axis_size("row")
    send = jnp.broadcast_to(block[None], (n_row,) + block.shape)
    received = lax.all_to_all(send, "row", 0, 0, tiled=True)
    return received.reshape((n_row * block.shape[0],) + block.shape[1:])


def local(
    tokens,
    image_sizes,
    slot_of,
    ln_gain,
    ln_bias,
    w_qkv,
    w_out,
    w_up,
    w_down,
    merge_gain,
    merge_bias,
    w_merge,
):
    n_col = lax.axis_size("col")
    n_row = lax.axis_size("row")
    row_index = lax.axis_index("row")
    tok_dev = tokens.shape[0]
    tok_row = tok_dev * n_col
    merged_row = tok_row // 4
    most = merged_row * 3 // 16
    sizes_here = lax.dynamic_index_in_dim(image_sizes, row_index, 0, keepdims=False)
    segments = segment_ids(sizes_here, tok_row)

    qkv_cols = w_qkv.shape[2]
    first = row_gather(jnp.concatenate([w_qkv[0], w_out[0].T], axis=1))
    up_cols = w_up.shape[2]
    second = row_gather(jnp.concatenate([w_up[0], w_down[0].T], axis=1))
    merge_full = row_gather(w_merge)
    qkv_full = first[:, :qkv_cols]
    out_t = first[:, qkv_cols:]
    up_full = second[:, :up_cols]
    down_t = second[:, up_cols:]
    contract_t = (((1,), (1,)), ((), ()))

    stream = lax.all_gather(tokens, "col", axis=0, tiled=True)
    normed_all = layer_norm(stream.astype(jnp.float32), ln_gain[0, 0], ln_bias[0, 0]).astype(
        jnp.bfloat16
    )
    qkv = jnp.dot(normed_all, qkv_full, preferred_element_type=jnp.float32)
    qkv = qkv.astype(jnp.bfloat16).reshape(tok_row, -1, 3, HEAD_DIM)
    context = attend(qkv, segments)
    attn_terms = lax.dot_general(
        context, out_t, contract_t, preferred_element_type=jnp.float32
    )
    attn_out = lax.psum(attn_terms.astype(jnp.bfloat16), "col").astype(jnp.float32)
    stream = (stream.astype(jnp.float32) + attn_out).astype(jnp.bfloat16)
    normed_mlp = layer_norm(stream.astype(jnp.float32), ln_gain[0, 1], ln_bias[0, 1]).astype(
        jnp.bfloat16
    )
    up_value = jnp.dot(normed_mlp, up_full, preferred_element_type=jnp.float32)
    hidden = jax.nn.gelu(up_value, approximate=False).astype(jnp.bfloat16)
    mlp_terms = lax.dot_general(
        hidden, down_t, contract_t, preferred_element_type=jnp.float32
    )
    mlp_out = lax.psum(mlp_terms.astype(jnp.bfloat16), "col").astype(jnp.float32)
    stream = (stream.astype(jnp.float32) + mlp_out).astype(jnp.bfloat16)
    merged = layer_norm(stream.astype(jnp.float32), merge_gain, merge_bias).astype(jnp.bfloat16)
    merged_all = merged.reshape(merged_row, 4 * D)
    out_dev = w_merge.shape[1]
    projected = jnp.dot(merged_all, merge_full, preferred_element_type=jnp.float32).astype(
        jnp.bfloat16
    )

    reqs = slot_of.shape[0]
    numbers = jnp.arange(reqs, dtype=jnp.int32)
    req_at_slot = jnp.sum(
        jnp.where(slot_of[None, :] == numbers[:, None], numbers[None, :], 0), axis=1
    )
    starts = jnp.cumsum(image_sizes, axis=1) - image_sizes
    sizes_flat = image_sizes.reshape(-1)
    inner = jnp.arange(most, dtype=jnp.int32)
    groups = jnp.arange(n_row, dtype=jnp.int32)
    my_dest = lax.dynamic_slice_in_dim(slot_of, row_index * IMG_ROW, IMG_ROW) // IMG_ROW
    my_starts = lax.dynamic_index_in_dim(starts, row_index, 0, keepdims=False)
    match = my_dest[None, :] == groups[:, None]
    start_to = jnp.sum(jnp.where(match, my_starts[None, :], 0), axis=1)
    padded = jnp.concatenate([projected, jnp.zeros((most, out_dev), projected.dtype)], axis=0)
    rows = jnp.clip(start_to[:, None] + inner[None, :], 0, padded.shape[0] - 1)
    send = jnp.take(padded, rows.reshape(-1), axis=0).reshape(n_row, most, out_dev)
    recv = lax.all_to_all(send, "row", 0, 0, tiled=True)

    request = lax.dynamic_slice_in_dim(req_at_slot, row_index * IMG_ROW, IMG_ROW)
    source = request // IMG_ROW
    taken = jnp.take(recv, source, axis=0)
    valid = inner[None, :] < sizes_flat[request][:, None]
    blocks = jnp.where(valid[:, :, None], taken, jnp.zeros_like(taken)).astype(jnp.float32)
    squares = jnp.sum(blocks * blocks, axis=(1, 2))
    peaks = jnp.max(jnp.abs(blocks), axis=(1, 2))
    stats = lax.all_gather(jnp.concatenate([squares, peaks]), "col", axis=0, tiled=False)
    squares = jnp.sum(stats[:, :IMG_ROW], axis=0)
    peaks = jnp.max(stats[:, IMG_ROW:], axis=0)
    slot_size = sizes_flat[request].astype(jnp.float32)
    req_norm = jnp.sqrt(squares / (slot_size * OUT) + 1e-06)
    merged_out = (
        (blocks / req_norm[:, None, None]).astype(jnp.bfloat16).reshape(IMG_ROW * most, out_dev)
    )
    return (merged_out, req_norm, peaks)


def solution(mesh):
    in_specs = (
        P(("row", "col"), None),
        P(),
        P(),
        P(),
        P(),
        P(None, "row", "col"),
        P(None, "col", "row"),
        P(None, "row", "col"),
        P(None, "col", "row"),
        P(),
        P(),
        P("row", "col"),
    )
    out_specs = (P("row", "col"), P("row"), P("row"))
    return jax.shard_map(local, mesh=mesh, in_specs=in_specs, out_specs=out_specs, check_vma=False)
```

```python
import jax
import jax.numpy as jnp
from jax import lax
from jax.sharding import PartitionSpec as P

D = 1280
HEAD_DIM = 80
OUT = 4096
IMG_ROW = 8


def layer_norm(values, gain, bias):
    center = jnp.mean(values, axis=-1, keepdims=True)
    shifted = values - center
    spread = jnp.mean(shifted * shifted, axis=-1, keepdims=True)
    return shifted * lax.rsqrt(spread + 1e-06) * gain + bias


def segment_ids(sizes_row, count):
    bounds = jnp.cumsum(sizes_row)
    merged_index = jnp.arange(count, dtype=jnp.int32) // 4
    return jnp.sum((merged_index[:, None] >= bounds[None, :]).astype(jnp.int32), axis=1)


def attend(qkv, segments):
    count = qkv.shape[0]
    width = min(512, count)
    query = qkv[:, :, 0]
    keys = qkv[:, :, 1]
    values = qkv[:, :, 2]
    results = []
    for offset in range(0, count, width):
        scores = jnp.einsum(
            "qhd,khd->hqk", query[offset : offset + width], keys, preferred_element_type=jnp.float32
        ) * HEAD_DIM ** (-0.5)
        same = segments[offset : offset + width, None] == segments[None, :]
        scores = jnp.where(same[None], scores, -1e30)
        peak = jnp.max(scores, axis=-1, keepdims=True)
        expo = jnp.exp(scores - peak)
        weights = (expo / jnp.sum(expo, axis=-1, keepdims=True)).astype(jnp.bfloat16)
        context = jnp.einsum("hqk,khd->qhd", weights, values, preferred_element_type=jnp.float32)
        results.append(context.astype(jnp.bfloat16).reshape(width, -1))
    return jnp.concatenate(results, axis=0)


def row_gather(block):
    n_row = lax.axis_size("row")
    send = jnp.broadcast_to(block[None], (n_row,) + block.shape)
    received = lax.all_to_all(send, "row", 0, 0, tiled=True)
    return received.reshape((n_row * block.shape[0],) + block.shape[1:])


def local(
    tokens,
    image_sizes,
    slot_of,
    ln_gain,
    ln_bias,
    w_qkv,
    w_out,
    w_up,
    w_down,
    merge_gain,
    merge_bias,
    w_merge,
):
    n_col = lax.axis_size("col")
    n_row = lax.axis_size("row")
    row_index = lax.axis_index("row")
    tok_dev = tokens.shape[0]
    tok_row = tok_dev * n_col
    merged_row = tok_row // 4
    most = merged_row * 3 // 16
    sizes_here = lax.dynamic_index_in_dim(image_sizes, row_index, 0, keepdims=False)
    segments = segment_ids(sizes_here, tok_row)

    qkv_cols = w_qkv.shape[2]
    first = row_gather(jnp.concatenate([w_qkv[0], w_out[0].T], axis=1))
    up_cols = w_up.shape[2]
    second = row_gather(jnp.concatenate([w_up[0], w_down[0].T], axis=1))
    merge_full = row_gather(w_merge)
    qkv_full = first[:, :qkv_cols]
    out_t = first[:, qkv_cols:]
    up_full = second[:, :up_cols]
    down_t = second[:, up_cols:]
    contract_t = (((1,), (1,)), ((), ()))

    stream = tokens
    normed = layer_norm(stream.astype(jnp.float32), ln_gain[0, 0], ln_bias[0, 0]).astype(
        jnp.bfloat16
    )
    normed_all = lax.all_gather(normed, "col", axis=0, tiled=True)
    qkv = jnp.dot(normed_all, qkv_full, preferred_element_type=jnp.float32)
    qkv = qkv.astype(jnp.bfloat16).reshape(tok_row, -1, 3, HEAD_DIM)
    context = attend(qkv, segments)
    head_cols = context.shape[1]
    pieces = lax.all_to_all(context.reshape(n_col, tok_dev, head_cols), "col", 0, 0, tiled=True)
    out_all = lax.all_gather(out_t.T, "col", axis=0, tiled=True)
    attn_out = jnp.zeros((tok_dev, D), jnp.float32)
    for c in range(n_col):
        term = jnp.dot(
            pieces[c],
            out_all[c * head_cols : (c + 1) * head_cols],
            preferred_element_type=jnp.float32,
        )
        attn_out = attn_out + term.astype(jnp.bfloat16).astype(jnp.float32)
    stream = (stream.astype(jnp.float32) + attn_out).astype(jnp.bfloat16)
    normed = layer_norm(stream.astype(jnp.float32), ln_gain[0, 1], ln_bias[0, 1]).astype(
        jnp.bfloat16
    )
    normed_mlp = lax.all_gather(normed, "col", axis=0, tiled=True)
    up_value = jnp.dot(normed_mlp, up_full, preferred_element_type=jnp.float32)
    hidden = jax.nn.gelu(up_value, approximate=False).astype(jnp.bfloat16)
    mlp_terms = lax.dot_general(
        hidden, down_t, contract_t, preferred_element_type=jnp.float32
    )
    mlp_out = lax.psum_scatter(
        mlp_terms.astype(jnp.bfloat16), "col", scatter_dimension=0, tiled=True
    ).astype(jnp.float32)
    stream = (stream.astype(jnp.float32) + mlp_out).astype(jnp.bfloat16)
    merged = layer_norm(stream.astype(jnp.float32), merge_gain, merge_bias).astype(jnp.bfloat16)
    merged = merged.reshape(tok_dev // 4, 4 * D)
    merged_all = lax.all_gather(merged, "col", axis=0, tiled=True)
    out_dev = w_merge.shape[1]
    projected = jnp.dot(merged_all, merge_full, preferred_element_type=jnp.float32).astype(
        jnp.bfloat16
    )

    reqs = slot_of.shape[0]
    numbers = jnp.arange(reqs, dtype=jnp.int32)
    req_at_slot = jnp.sum(
        jnp.where(slot_of[None, :] == numbers[:, None], numbers[None, :], 0), axis=1
    )
    starts = jnp.cumsum(image_sizes, axis=1) - image_sizes
    sizes_flat = image_sizes.reshape(-1)
    inner = jnp.arange(most, dtype=jnp.int32)
    groups = jnp.arange(n_row, dtype=jnp.int32)
    my_dest = lax.dynamic_slice_in_dim(slot_of, row_index * IMG_ROW, IMG_ROW) // IMG_ROW
    my_starts = lax.dynamic_index_in_dim(starts, row_index, 0, keepdims=False)
    match = my_dest[None, :] == groups[:, None]
    start_to = jnp.sum(jnp.where(match, my_starts[None, :], 0), axis=1)
    padded = jnp.concatenate([projected, jnp.zeros((most, out_dev), projected.dtype)], axis=0)
    rows = jnp.clip(start_to[:, None] + inner[None, :], 0, padded.shape[0] - 1)
    send = jnp.take(padded, rows.reshape(-1), axis=0).reshape(n_row, most, out_dev)
    recv = lax.all_to_all(send, "row", 0, 0, tiled=True)

    request = lax.dynamic_slice_in_dim(req_at_slot, row_index * IMG_ROW, IMG_ROW)
    source = request // IMG_ROW
    taken = jnp.take(recv, source, axis=0)
    valid = inner[None, :] < sizes_flat[request][:, None]
    blocks = jnp.where(valid[:, :, None], taken, jnp.zeros_like(taken)).astype(jnp.float32)
    squares = jnp.sum(blocks * blocks, axis=(1, 2))
    peaks = jnp.max(jnp.abs(blocks), axis=(1, 2))
    stats = lax.all_gather(jnp.concatenate([squares, peaks]), "col", axis=0, tiled=False)
    squares = jnp.sum(stats[:, :IMG_ROW], axis=0)
    peaks = jnp.max(stats[:, IMG_ROW:], axis=0)
    slot_size = sizes_flat[request].astype(jnp.float32)
    req_norm = jnp.sqrt(squares / (slot_size * OUT) + 1e-06)
    merged_out = (
        (blocks / req_norm[:, None, None]).astype(jnp.bfloat16).reshape(IMG_ROW * most, out_dev)
    )
    return (merged_out, req_norm, peaks)


def solution(mesh):
    in_specs = (
        P(("row", "col"), None),
        P(),
        P(),
        P(),
        P(),
        P(None, "row", "col"),
        P(None, "col", "row"),
        P(None, "row", "col"),
        P(None, "col", "row"),
        P(),
        P(),
        P("row", "col"),
    )
    out_specs = (P("row", "col"), P("row"), P("row"))
    return jax.shard_map(local, mesh=mesh, in_specs=in_specs, out_specs=out_specs, check_vma=False)
```

```python
import jax
import jax.numpy as jnp
from jax import lax
from jax.sharding import PartitionSpec as P

D = 1280
HEAD_DIM = 80
OUT = 4096
IMG_ROW = 8


def layer_norm(values, gain, bias):
    center = jnp.mean(values, axis=-1, keepdims=True)
    shifted = values - center
    spread = jnp.mean(shifted * shifted, axis=-1, keepdims=True)
    return shifted * lax.rsqrt(spread + 1e-06) * gain + bias


def segment_ids(sizes_row, count):
    bounds = jnp.cumsum(sizes_row)
    merged_index = jnp.arange(count, dtype=jnp.int32) // 4
    return jnp.sum((merged_index[:, None] >= bounds[None, :]).astype(jnp.int32), axis=1)


def attend(qkv, segments):
    count = qkv.shape[0]
    width = min(512, count)
    query = qkv[:, :, 0]
    keys = qkv[:, :, 1]
    values = qkv[:, :, 2]
    results = []
    for offset in range(0, count, width):
        scores = jnp.einsum(
            "qhd,khd->hqk", query[offset : offset + width], keys, preferred_element_type=jnp.float32
        ) * HEAD_DIM ** (-0.5)
        same = segments[offset : offset + width, None] == segments[None, :]
        scores = jnp.where(same[None], scores, -1e30)
        peak = jnp.max(scores, axis=-1, keepdims=True)
        expo = jnp.exp(scores - peak)
        weights = (expo / jnp.sum(expo, axis=-1, keepdims=True)).astype(jnp.bfloat16)
        context = jnp.einsum("hqk,khd->qhd", weights, values, preferred_element_type=jnp.float32)
        results.append(context.astype(jnp.bfloat16).reshape(width, -1))
    return jnp.concatenate(results, axis=0)


def row_gather(block):
    n_row = lax.axis_size("row")
    send = jnp.broadcast_to(block[None], (n_row,) + block.shape)
    received = lax.all_to_all(send, "row", 0, 0, tiled=True)
    return received.reshape((n_row * block.shape[0],) + block.shape[1:])


def local(
    tokens,
    image_sizes,
    slot_of,
    ln_gain,
    ln_bias,
    w_qkv,
    w_out,
    w_up,
    w_down,
    merge_gain,
    merge_bias,
    w_merge,
):
    n_col = lax.axis_size("col")
    n_row = lax.axis_size("row")
    row_index = lax.axis_index("row")
    tok_dev = tokens.shape[0]
    tok_row = tok_dev * n_col
    merged_row = tok_row // 4
    most = merged_row * 3 // 16
    sizes_here = lax.dynamic_index_in_dim(image_sizes, row_index, 0, keepdims=False)
    segments = segment_ids(sizes_here, tok_row)

    qkv_cols = w_qkv.shape[2]
    first = row_gather(jnp.concatenate([w_qkv[0], w_out[0].T], axis=1))
    up_cols = w_up.shape[2]
    second = row_gather(jnp.concatenate([w_up[0], w_down[0].T], axis=1))
    merge_full = row_gather(w_merge)
    qkv_full = first[:, :qkv_cols]
    out_t = first[:, qkv_cols:]
    up_full = second[:, :up_cols]
    down_t = second[:, up_cols:]
    contract_t = (((1,), (1,)), ((), ()))

    stream = tokens
    normed = layer_norm(stream.astype(jnp.float32), ln_gain[0, 0], ln_bias[0, 0]).astype(
        jnp.bfloat16
    )
    normed_all = lax.all_gather(normed, "col", axis=0, tiled=True)
    qkv = jnp.dot(normed_all, qkv_full, preferred_element_type=jnp.float32)
    qkv = qkv.astype(jnp.bfloat16).reshape(tok_row, -1, 3, HEAD_DIM)
    context = attend(qkv, segments)
    head_cols = context.shape[1]
    col_index = lax.axis_index("col")
    out_all = lax.all_gather(out_t.T, "col", axis=0, tiled=True)
    attn_out = jnp.zeros((tok_dev, D), jnp.float32)
    for shift in range(n_col):
        target = (col_index + shift) % n_col
        block = lax.dynamic_slice_in_dim(context, target * tok_dev, tok_dev, 0)
        if shift:
            pairs = [(i, (i + shift) % n_col) for i in range(n_col)]
            block = lax.ppermute(block, "col", pairs)
        source = (col_index - shift) % n_col
        rows = lax.dynamic_slice_in_dim(out_all, source * head_cols, head_cols, 0)
        term = jnp.dot(block, rows, preferred_element_type=jnp.float32)
        attn_out = attn_out + term.astype(jnp.bfloat16).astype(jnp.float32)
    stream = (stream.astype(jnp.float32) + attn_out).astype(jnp.bfloat16)
    normed = layer_norm(stream.astype(jnp.float32), ln_gain[0, 1], ln_bias[0, 1]).astype(
        jnp.bfloat16
    )
    normed_mlp = lax.all_gather(normed, "col", axis=0, tiled=True)
    up_value = jnp.dot(normed_mlp, up_full, preferred_element_type=jnp.float32)
    hidden = jax.nn.gelu(up_value, approximate=False).astype(jnp.bfloat16)
    mlp_terms = lax.dot_general(
        hidden, down_t, contract_t, preferred_element_type=jnp.float32
    )
    mlp_out = lax.psum_scatter(
        mlp_terms.astype(jnp.bfloat16), "col", scatter_dimension=0, tiled=True
    ).astype(jnp.float32)
    stream = (stream.astype(jnp.float32) + mlp_out).astype(jnp.bfloat16)
    merged = layer_norm(stream.astype(jnp.float32), merge_gain, merge_bias).astype(jnp.bfloat16)
    merged = merged.reshape(tok_dev // 4, 4 * D)
    merged_all = lax.all_gather(merged, "col", axis=0, tiled=True)
    out_dev = w_merge.shape[1]
    projected = jnp.dot(merged_all, merge_full, preferred_element_type=jnp.float32).astype(
        jnp.bfloat16
    )

    reqs = slot_of.shape[0]
    numbers = jnp.arange(reqs, dtype=jnp.int32)
    req_at_slot = jnp.sum(
        jnp.where(slot_of[None, :] == numbers[:, None], numbers[None, :], 0), axis=1
    )
    starts = jnp.cumsum(image_sizes, axis=1) - image_sizes
    sizes_flat = image_sizes.reshape(-1)
    inner = jnp.arange(most, dtype=jnp.int32)
    groups = jnp.arange(n_row, dtype=jnp.int32)
    my_dest = lax.dynamic_slice_in_dim(slot_of, row_index * IMG_ROW, IMG_ROW) // IMG_ROW
    my_starts = lax.dynamic_index_in_dim(starts, row_index, 0, keepdims=False)
    match = my_dest[None, :] == groups[:, None]
    start_to = jnp.sum(jnp.where(match, my_starts[None, :], 0), axis=1)
    padded = jnp.concatenate([projected, jnp.zeros((most, out_dev), projected.dtype)], axis=0)
    rows = jnp.clip(start_to[:, None] + inner[None, :], 0, padded.shape[0] - 1)
    send = jnp.take(padded, rows.reshape(-1), axis=0).reshape(n_row, most, out_dev)
    recv = lax.all_to_all(send, "row", 0, 0, tiled=True)

    owner = segment_ids(sizes_here, merged_row * 4)[::4]
    own = owner[:, None] == jnp.arange(IMG_ROW, dtype=jnp.int32)[None, :]
    proj32 = projected.astype(jnp.float32)
    row_sq = jnp.sum(proj32 * proj32, axis=1)
    row_peak = jnp.max(jnp.abs(proj32), axis=1)
    part_sq = jnp.sum(jnp.where(own, row_sq[:, None], 0.0), axis=0)
    part_peak = jnp.max(jnp.where(own, row_peak[:, None], 0.0), axis=0)
    col_stats = lax.all_gather(jnp.concatenate([part_sq, part_peak]), "col", axis=0, tiled=False)
    group_stats = jnp.concatenate(
        [jnp.sum(col_stats[:, :IMG_ROW], axis=0), jnp.max(col_stats[:, IMG_ROW:], axis=0)]
    )
    all_stats = lax.all_gather(group_stats, "row", axis=0, tiled=False)
    req_sq = all_stats[:, :IMG_ROW].reshape(-1)
    req_peak = all_stats[:, IMG_ROW:].reshape(-1)

    request = lax.dynamic_slice_in_dim(req_at_slot, row_index * IMG_ROW, IMG_ROW)
    source = request // IMG_ROW
    taken = jnp.take(recv, source, axis=0)
    valid = inner[None, :] < sizes_flat[request][:, None]
    blocks = jnp.where(valid[:, :, None], taken, jnp.zeros_like(taken)).astype(jnp.float32)
    squares = req_sq[request]
    peaks = req_peak[request]
    slot_size = sizes_flat[request].astype(jnp.float32)
    req_norm = jnp.sqrt(squares / (slot_size * OUT) + 1e-06)
    merged_out = (
        (blocks / req_norm[:, None, None]).astype(jnp.bfloat16).reshape(IMG_ROW * most, out_dev)
    )
    return (merged_out, req_norm, peaks)


def solution(mesh):
    in_specs = (
        P(("row", "col"), None),
        P(),
        P(),
        P(),
        P(),
        P(None, "row", "col"),
        P(None, "col", "row"),
        P(None, "row", "col"),
        P(None, "col", "row"),
        P(),
        P(),
        P("row", "col"),
    )
    out_specs = (P("row", "col"), P("row"), P("row"))
    return jax.shard_map(local, mesh=mesh, in_specs=in_specs, out_specs=out_specs, check_vma=False)
```

```python
import jax
import jax.numpy as jnp
from jax import lax
from jax.sharding import PartitionSpec as P


D = 1280
HEAD_DIM = 80
OUT = 4096
IMG_ROW = 8


def layer_norm(values, gain, bias):
    center = jnp.mean(values, axis=-1, keepdims=True)
    shifted = values - center
    spread = jnp.mean(shifted * shifted, axis=-1, keepdims=True)
    return shifted * lax.rsqrt(spread + 1e-06) * gain + bias


def segment_ids(sizes_row, count):
    bounds = jnp.cumsum(sizes_row)
    merged_index = jnp.arange(count, dtype=jnp.int32) // 4
    return jnp.sum((merged_index[:, None] >= bounds[None, :]).astype(jnp.int32), axis=1)


def attend(qkv, segments):
    count = qkv.shape[0]
    width = min(512, count)
    query = qkv[:, :, 0]
    keys = qkv[:, :, 1]
    values = qkv[:, :, 2]
    results = []
    for offset in range(0, count, width):
        scores = jnp.einsum(
            "qhd,khd->hqk", query[offset : offset + width], keys, preferred_element_type=jnp.float32
        ) * HEAD_DIM ** (-0.5)
        same = segments[offset : offset + width, None] == segments[None, :]
        scores = jnp.where(same[None], scores, -1e30)
        peak = jnp.max(scores, axis=-1, keepdims=True)
        expo = jnp.exp(scores - peak)
        weights = (expo / jnp.sum(expo, axis=-1, keepdims=True)).astype(jnp.bfloat16)
        context = jnp.einsum("hqk,khd->qhd", weights, values, preferred_element_type=jnp.float32)
        results.append(context.astype(jnp.bfloat16).reshape(width, -1))
    return jnp.concatenate(results, axis=0)


def row_gather(block):
    n_row = lax.axis_size("row")
    send = jnp.broadcast_to(block[None], (n_row,) + block.shape)
    received = lax.all_to_all(send, "row", 0, 0, tiled=True)
    return received.reshape((n_row * block.shape[0],) + block.shape[1:])


def local(
    tokens,
    image_sizes,
    slot_of,
    ln_gain,
    ln_bias,
    w_qkv,
    w_out,
    w_up,
    w_down,
    merge_gain,
    merge_bias,
    w_merge,
):
    n_col = lax.axis_size("col")
    n_row = lax.axis_size("row")
    row_index = lax.axis_index("row")
    tok_dev = tokens.shape[0]
    tok_row = tok_dev * n_col
    merged_row = tok_row // 4
    most = merged_row * 3 // 16
    sizes_here = lax.dynamic_index_in_dim(image_sizes, row_index, 0, keepdims=False)
    segments = segment_ids(sizes_here, tok_row)

    qkv_cols = w_qkv.shape[2]
    first = row_gather(jnp.concatenate([w_qkv[0], w_out[0].T], axis=1))
    up_cols = w_up.shape[2]
    second = row_gather(jnp.concatenate([w_up[0], w_down[0].T], axis=1))
    merge_full = row_gather(w_merge)
    qkv_full = first[:, :qkv_cols]
    out_t = first[:, qkv_cols:]
    up_full = second[:, :up_cols]
    down_t = second[:, up_cols:]
    contract_t = (((1,), (1,)), ((), ()))

    stream = tokens
    normed = layer_norm(stream.astype(jnp.float32), ln_gain[0, 0], ln_bias[0, 0]).astype(
        jnp.bfloat16
    )
    normed_all = lax.all_gather(normed, "col", axis=0, tiled=True)
    qkv = jnp.dot(normed_all, qkv_full, preferred_element_type=jnp.float32)
    qkv = qkv.astype(jnp.bfloat16).reshape(tok_row, -1, 3, HEAD_DIM)
    context = attend(qkv, segments)
    head_cols = context.shape[1]
    col_index = lax.axis_index("col")
    out_all = lax.all_gather(out_t.T, "col", axis=0, tiled=True)
    attn_out = jnp.zeros((tok_dev, D), jnp.float32)
    for shift in range(n_col):
        target = (col_index + shift) % n_col
        block = lax.dynamic_slice_in_dim(context, target * tok_dev, tok_dev, 0)
        if shift:
            pairs = [(i, (i + shift) % n_col) for i in range(n_col)]
            block = lax.ppermute(block, "col", pairs)
        source = (col_index - shift) % n_col
        rows = lax.dynamic_slice_in_dim(out_all, source * head_cols, head_cols, 0)
        term = jnp.dot(block, rows, preferred_element_type=jnp.float32)
        attn_out = attn_out + term.astype(jnp.bfloat16).astype(jnp.float32)
    stream = (stream.astype(jnp.float32) + attn_out).astype(jnp.bfloat16)
    normed = layer_norm(stream.astype(jnp.float32), ln_gain[0, 1], ln_bias[0, 1]).astype(
        jnp.bfloat16
    )
    normed_mlp = lax.all_gather(normed, "col", axis=0, tiled=True)
    up_value = jnp.dot(normed_mlp, up_full, preferred_element_type=jnp.float32)
    hidden = jax.nn.gelu(up_value, approximate=False).astype(jnp.bfloat16)
    mlp_terms = lax.dot_general(
        hidden, down_t, contract_t, preferred_element_type=jnp.float32
    )
    mlp_out = lax.psum_scatter(
        mlp_terms.astype(jnp.bfloat16), "col", scatter_dimension=0, tiled=True
    ).astype(jnp.float32)
    stream = (stream.astype(jnp.float32) + mlp_out).astype(jnp.bfloat16)
    merged = layer_norm(stream.astype(jnp.float32), merge_gain, merge_bias).astype(jnp.bfloat16)
    merged = merged.reshape(tok_dev // 4, 4 * D)
    merged_all = lax.all_gather(merged, "col", axis=0, tiled=True)
    out_dev = w_merge.shape[1]
    projected = jnp.dot(merged_all, merge_full, preferred_element_type=jnp.float32).astype(
        jnp.bfloat16
    )

    reqs = slot_of.shape[0]
    numbers = jnp.arange(reqs, dtype=jnp.int32)
    req_at_slot = jnp.sum(
        jnp.where(slot_of[None, :] == numbers[:, None], numbers[None, :], 0), axis=1
    )
    starts = jnp.cumsum(image_sizes, axis=1) - image_sizes
    sizes_flat = image_sizes.reshape(-1)
    inner = jnp.arange(most, dtype=jnp.int32)
    groups = jnp.arange(n_row, dtype=jnp.int32)
    my_dest = lax.dynamic_slice_in_dim(slot_of, row_index * IMG_ROW, IMG_ROW) // IMG_ROW
    my_starts = lax.dynamic_index_in_dim(starts, row_index, 0, keepdims=False)
    match = my_dest[None, :] == groups[:, None]
    start_to = jnp.sum(jnp.where(match, my_starts[None, :], 0), axis=1)
    padded = jnp.concatenate([projected, jnp.zeros((most, out_dev), projected.dtype)], axis=0)
    rows = jnp.clip(start_to[:, None] + inner[None, :], 0, padded.shape[0] - 1)
    send = jnp.take(padded, rows.reshape(-1), axis=0).reshape(n_row, most, out_dev)
    recv = lax.all_to_all(send, "row", 0, 0, tiled=True)

    request = lax.dynamic_slice_in_dim(req_at_slot, row_index * IMG_ROW, IMG_ROW)
    source = request // IMG_ROW
    taken = jnp.take(recv, source, axis=0)
    valid = inner[None, :] < sizes_flat[request][:, None]
    blocks = jnp.where(valid[:, :, None], taken, jnp.zeros_like(taken)).astype(jnp.float32)
    squares = jnp.sum(blocks * blocks, axis=(1, 2))
    peaks = jnp.max(jnp.abs(blocks), axis=(1, 2))
    stats = lax.all_gather(jnp.concatenate([squares, peaks]), "col", axis=0, tiled=False)
    squares = jnp.sum(stats[:, :IMG_ROW], axis=0)
    peaks = jnp.max(stats[:, IMG_ROW:], axis=0)
    slot_size = sizes_flat[request].astype(jnp.float32)
    req_norm = jnp.sqrt(squares / (slot_size * OUT) + 1e-06)
    merged_out = (
        (blocks / req_norm[:, None, None]).astype(jnp.bfloat16).reshape(IMG_ROW * most, out_dev)
    )
    return (merged_out, req_norm, peaks)


def solution(mesh):
    in_specs = (
        P(("row", "col"), None),
        P(),
        P(),
        P(),
        P(),
        P(None, "row", "col"),
        P(None, "col", "row"),
        P(None, "row", "col"),
        P(None, "col", "row"),
        P(),
        P(),
        P("row", "col"),
    )
    out_specs = (P("row", "col"), P("row"), P("row"))
    return jax.shard_map(local, mesh=mesh, in_specs=in_specs, out_specs=out_specs, check_vma=False)
```

```python
import jax
import jax.numpy as jnp
from jax import lax
from jax.sharding import PartitionSpec as P


D = 1280
HEAD_DIM = 80
OUT = 4096
IMG_ROW = 8


def layer_norm(values, gain, bias):
    center = jnp.mean(values, axis=-1, keepdims=True)
    shifted = values - center
    spread = jnp.mean(shifted * shifted, axis=-1, keepdims=True)
    return shifted * lax.rsqrt(spread + 1e-06) * gain + bias


def segment_ids(sizes_row, count):
    bounds = jnp.cumsum(sizes_row)
    merged_index = jnp.arange(count, dtype=jnp.int32) // 4
    return jnp.sum((merged_index[:, None] >= bounds[None, :]).astype(jnp.int32), axis=1)


def attend(qkv, segments):
    count = qkv.shape[0]
    width = min(512, count)
    query = qkv[:, :, 0]
    keys = qkv[:, :, 1]
    values = qkv[:, :, 2]
    results = []
    for offset in range(0, count, width):
        scores = jnp.einsum(
            "qhd,khd->hqk", query[offset : offset + width], keys, preferred_element_type=jnp.float32
        ) * HEAD_DIM ** (-0.5)
        same = segments[offset : offset + width, None] == segments[None, :]
        scores = jnp.where(same[None], scores, -1e30)
        peak = jnp.max(scores, axis=-1, keepdims=True)
        expo = jnp.exp(scores - peak)
        weights = (expo / jnp.sum(expo, axis=-1, keepdims=True)).astype(jnp.bfloat16)
        context = jnp.einsum("hqk,khd->qhd", weights, values, preferred_element_type=jnp.float32)
        results.append(context.astype(jnp.bfloat16).reshape(width, -1))
    return jnp.concatenate(results, axis=0)


def row_gather(block):
    n_row = lax.axis_size("row")
    send = jnp.broadcast_to(block[None], (n_row,) + block.shape)
    received = lax.all_to_all(send, "row", 0, 0, tiled=True)
    return received.reshape((n_row * block.shape[0],) + block.shape[1:])


def local(
    tokens,
    image_sizes,
    slot_of,
    ln_gain,
    ln_bias,
    w_qkv,
    w_out,
    w_up,
    w_down,
    merge_gain,
    merge_bias,
    w_merge,
):
    n_col = lax.axis_size("col")
    n_row = lax.axis_size("row")
    row_index = lax.axis_index("row")
    tok_dev = tokens.shape[0]
    tok_row = tok_dev * n_col
    merged_row = tok_row // 4
    most = merged_row * 3 // 16
    sizes_here = lax.dynamic_index_in_dim(image_sizes, row_index, 0, keepdims=False)
    segments = segment_ids(sizes_here, tok_row)

    qkv_cols = w_qkv.shape[2]
    first = row_gather(jnp.concatenate([w_qkv[0], w_out[0].T], axis=1))
    up_cols = w_up.shape[2]
    second = row_gather(jnp.concatenate([w_up[0], w_down[0].T], axis=1))
    merge_full = row_gather(w_merge)
    qkv_full = first[:, :qkv_cols]
    out_t = first[:, qkv_cols:]
    up_full = second[:, :up_cols]
    down_t = second[:, up_cols:]
    contract_t = (((1,), (1,)), ((), ()))

    stream = tokens
    normed = layer_norm(stream.astype(jnp.float32), ln_gain[0, 0], ln_bias[0, 0]).astype(
        jnp.bfloat16
    )
    normed_all = lax.all_gather(normed, "col", axis=0, tiled=True)
    qkv = jnp.dot(normed_all, qkv_full, preferred_element_type=jnp.float32)
    qkv = qkv.astype(jnp.bfloat16).reshape(tok_row, -1, 3, HEAD_DIM)
    context = attend(qkv, segments)
    head_cols = context.shape[1]
    col_index = lax.axis_index("col")
    out_all = lax.all_gather(out_t.T, "col", axis=0, tiled=True)
    attn_out = jnp.zeros((tok_dev, D), jnp.float32)
    for shift in range(n_col):
        target = (col_index + shift) % n_col
        block = lax.dynamic_slice_in_dim(context, target * tok_dev, tok_dev, 0)
        if shift:
            pairs = [(i, (i + shift) % n_col) for i in range(n_col)]
            block = lax.ppermute(block, "col", pairs)
        source = (col_index - shift) % n_col
        rows = lax.dynamic_slice_in_dim(out_all, source * head_cols, head_cols, 0)
        term = jnp.dot(block, rows, preferred_element_type=jnp.float32)
        attn_out = attn_out + term.astype(jnp.bfloat16).astype(jnp.float32)
    stream = (stream.astype(jnp.float32) + attn_out).astype(jnp.bfloat16)
    normed = layer_norm(stream.astype(jnp.float32), ln_gain[0, 1], ln_bias[0, 1]).astype(
        jnp.bfloat16
    )
    normed_mlp = lax.all_gather(normed, "col", axis=0, tiled=True)
    up_value = jnp.dot(normed_mlp, up_full, preferred_element_type=jnp.float32)
    hidden = jax.nn.gelu(up_value, approximate=False).astype(jnp.bfloat16)
    mlp_terms = lax.dot_general(
        hidden, down_t, contract_t, preferred_element_type=jnp.float32
    )
    mlp_terms = mlp_terms.astype(jnp.bfloat16)
    split = D // 2
    head_sum = lax.psum_scatter(
        mlp_terms[:, :split], "col", scatter_dimension=0, tiled=True
    ).astype(jnp.float32)
    tail_terms = mlp_terms[:, split:]
    tail_sum = jnp.zeros((tok_dev, D - split), jnp.float32)
    for shift in range(n_col):
        target = (col_index + shift) % n_col
        block = lax.dynamic_slice_in_dim(tail_terms, target * tok_dev, tok_dev, 0)
        if shift:
            pairs = [(i, (i + shift) % n_col) for i in range(n_col)]
            block = lax.ppermute(block, "col", pairs)
        tail_sum = tail_sum + block.astype(jnp.float32)
    mlp_out = jnp.concatenate([head_sum, tail_sum], axis=1)
    stream = (stream.astype(jnp.float32) + mlp_out).astype(jnp.bfloat16)
    merged = layer_norm(stream.astype(jnp.float32), merge_gain, merge_bias).astype(jnp.bfloat16)
    merged = merged.reshape(tok_dev // 4, 4 * D)
    merged_all = lax.all_gather(merged, "col", axis=0, tiled=True)
    out_dev = w_merge.shape[1]
    projected = jnp.dot(merged_all, merge_full, preferred_element_type=jnp.float32).astype(
        jnp.bfloat16
    )

    reqs = slot_of.shape[0]
    numbers = jnp.arange(reqs, dtype=jnp.int32)
    req_at_slot = jnp.sum(
        jnp.where(slot_of[None, :] == numbers[:, None], numbers[None, :], 0), axis=1
    )
    starts = jnp.cumsum(image_sizes, axis=1) - image_sizes
    sizes_flat = image_sizes.reshape(-1)
    inner = jnp.arange(most, dtype=jnp.int32)
    groups = jnp.arange(n_row, dtype=jnp.int32)
    my_dest = lax.dynamic_slice_in_dim(slot_of, row_index * IMG_ROW, IMG_ROW) // IMG_ROW
    my_starts = lax.dynamic_index_in_dim(starts, row_index, 0, keepdims=False)
    match = my_dest[None, :] == groups[:, None]
    start_to = jnp.sum(jnp.where(match, my_starts[None, :], 0), axis=1)
    padded = jnp.concatenate([projected, jnp.zeros((most, out_dev), projected.dtype)], axis=0)
    rows = jnp.clip(start_to[:, None] + inner[None, :], 0, padded.shape[0] - 1)
    send = jnp.take(padded, rows.reshape(-1), axis=0).reshape(n_row, most, out_dev)
    recv = lax.all_to_all(send, "row", 0, 0, tiled=True)

    request = lax.dynamic_slice_in_dim(req_at_slot, row_index * IMG_ROW, IMG_ROW)
    source = request // IMG_ROW
    taken = jnp.take(recv, source, axis=0)
    valid = inner[None, :] < sizes_flat[request][:, None]
    blocks = jnp.where(valid[:, :, None], taken, jnp.zeros_like(taken)).astype(jnp.float32)
    squares = jnp.sum(blocks * blocks, axis=(1, 2))
    peaks = jnp.max(jnp.abs(blocks), axis=(1, 2))
    stats = lax.all_gather(jnp.concatenate([squares, peaks]), "col", axis=0, tiled=False)
    squares = jnp.sum(stats[:, :IMG_ROW], axis=0)
    peaks = jnp.max(stats[:, IMG_ROW:], axis=0)
    slot_size = sizes_flat[request].astype(jnp.float32)
    req_norm = jnp.sqrt(squares / (slot_size * OUT) + 1e-06)
    merged_out = (
        (blocks / req_norm[:, None, None]).astype(jnp.bfloat16).reshape(IMG_ROW * most, out_dev)
    )
    return (merged_out, req_norm, peaks)


def solution(mesh):
    in_specs = (
        P(("row", "col"), None),
        P(),
        P(),
        P(),
        P(),
        P(None, "row", "col"),
        P(None, "col", "row"),
        P(None, "row", "col"),
        P(None, "col", "row"),
        P(),
        P(),
        P("row", "col"),
    )
    out_specs = (P("row", "col"), P("row"), P("row"))
    return jax.shard_map(local, mesh=mesh, in_specs=in_specs, out_specs=out_specs, check_vma=False)
```

```python
import jax
import jax.numpy as jnp
from jax import lax
from jax.sharding import PartitionSpec as P


D = 1280
HEAD_DIM = 80
OUT = 4096
IMG_ROW = 8


def layer_norm(values, gain, bias):
    center = jnp.mean(values, axis=-1, keepdims=True)
    shifted = values - center
    spread = jnp.mean(shifted * shifted, axis=-1, keepdims=True)
    return shifted * lax.rsqrt(spread + 1e-06) * gain + bias


def segment_ids(sizes_row, count):
    bounds = jnp.cumsum(sizes_row)
    merged_index = jnp.arange(count, dtype=jnp.int32) // 4
    return jnp.sum((merged_index[:, None] >= bounds[None, :]).astype(jnp.int32), axis=1)


def attend(qkv, segments):
    count = qkv.shape[0]
    width = min(512, count)
    query = qkv[:, :, 0]
    keys = qkv[:, :, 1]
    values = qkv[:, :, 2]
    results = []
    for offset in range(0, count, width):
        scores = jnp.einsum(
            "qhd,khd->hqk", query[offset : offset + width], keys, preferred_element_type=jnp.float32
        ) * HEAD_DIM ** (-0.5)
        same = segments[offset : offset + width, None] == segments[None, :]
        scores = jnp.where(same[None], scores, -1e30)
        peak = jnp.max(scores, axis=-1, keepdims=True)
        expo = jnp.exp(scores - peak)
        weights = (expo / jnp.sum(expo, axis=-1, keepdims=True)).astype(jnp.bfloat16)
        context = jnp.einsum("hqk,khd->qhd", weights, values, preferred_element_type=jnp.float32)
        results.append(context.astype(jnp.bfloat16).reshape(width, -1))
    return jnp.concatenate(results, axis=0)


def row_gather(block):
    n_row = lax.axis_size("row")
    send = jnp.broadcast_to(block[None], (n_row,) + block.shape)
    received = lax.all_to_all(send, "row", 0, 0, tiled=True)
    return received.reshape((n_row * block.shape[0],) + block.shape[1:])


def local(
    tokens,
    image_sizes,
    slot_of,
    ln_gain,
    ln_bias,
    w_qkv,
    w_out,
    w_up,
    w_down,
    merge_gain,
    merge_bias,
    w_merge,
):
    n_col = lax.axis_size("col")
    n_row = lax.axis_size("row")
    row_index = lax.axis_index("row")
    tok_dev = tokens.shape[0]
    tok_row = tok_dev * n_col
    merged_row = tok_row // 4
    most = merged_row * 3 // 16
    sizes_here = lax.dynamic_index_in_dim(image_sizes, row_index, 0, keepdims=False)
    segments = segment_ids(sizes_here, tok_row)

    qkv_cols = w_qkv.shape[2]
    first = row_gather(jnp.concatenate([w_qkv[0], w_out[0].T], axis=1))
    up_cols = w_up.shape[2]
    second = row_gather(jnp.concatenate([w_up[0], w_down[0].T], axis=1))
    merge_full = row_gather(w_merge)
    qkv_full = first[:, :qkv_cols]
    out_t = first[:, qkv_cols:]
    up_full = second[:, :up_cols]
    down_t = second[:, up_cols:]
    contract_t = (((1,), (1,)), ((), ()))

    stream = tokens
    normed = layer_norm(stream.astype(jnp.float32), ln_gain[0, 0], ln_bias[0, 0]).astype(
        jnp.bfloat16
    )
    normed_all = lax.all_gather(normed, "col", axis=0, tiled=True)
    qkv = jnp.dot(normed_all, qkv_full, preferred_element_type=jnp.float32)
    qkv = qkv.astype(jnp.bfloat16).reshape(tok_row, -1, 3, HEAD_DIM)
    context = attend(qkv, segments)
    head_cols = context.shape[1]
    col_index = lax.axis_index("col")
    out_all = lax.all_gather(out_t.T, "col", axis=0, tiled=True)
    attn_out = jnp.zeros((tok_dev, D), jnp.float32)
    for shift in range(n_col):
        target = (col_index + shift) % n_col
        block = lax.dynamic_slice_in_dim(context, target * tok_dev, tok_dev, 0)
        if shift:
            pairs = [(i, (i + shift) % n_col) for i in range(n_col)]
            block = lax.ppermute(block, "col", pairs)
        source = (col_index - shift) % n_col
        rows = lax.dynamic_slice_in_dim(out_all, source * head_cols, head_cols, 0)
        term = jnp.dot(block, rows, preferred_element_type=jnp.float32)
        attn_out = attn_out + term.astype(jnp.bfloat16).astype(jnp.float32)
    stream = (stream.astype(jnp.float32) + attn_out).astype(jnp.bfloat16)
    normed = layer_norm(stream.astype(jnp.float32), ln_gain[0, 1], ln_bias[0, 1]).astype(
        jnp.bfloat16
    )
    normed_mlp = lax.all_gather(normed, "col", axis=0, tiled=True)
    up_value = jnp.dot(normed_mlp, up_full, preferred_element_type=jnp.float32)
    hidden = jax.nn.gelu(up_value, approximate=False).astype(jnp.bfloat16)
    mlp_terms = lax.dot_general(
        hidden, down_t, contract_t, preferred_element_type=jnp.float32
    )
    mlp_terms = mlp_terms.astype(jnp.bfloat16)
    mlp_out = jnp.zeros((tok_dev, D), jnp.float32)
    for shift in range(n_col):
        target = (col_index + shift) % n_col
        block = lax.dynamic_slice_in_dim(mlp_terms, target * tok_dev, tok_dev, 0)
        if shift:
            pairs = [(i, (i + shift) % n_col) for i in range(n_col)]
            block = lax.ppermute(block, "col", pairs)
        mlp_out = mlp_out + block.astype(jnp.float32)
    stream = (stream.astype(jnp.float32) + mlp_out).astype(jnp.bfloat16)
    merged = layer_norm(stream.astype(jnp.float32), merge_gain, merge_bias).astype(jnp.bfloat16)
    merged = merged.reshape(tok_dev // 4, 4 * D)
    merged_all = lax.all_gather(merged, "col", axis=0, tiled=True)
    out_dev = w_merge.shape[1]
    projected = jnp.dot(merged_all, merge_full, preferred_element_type=jnp.float32).astype(
        jnp.bfloat16
    )

    reqs = slot_of.shape[0]
    numbers = jnp.arange(reqs, dtype=jnp.int32)
    req_at_slot = jnp.sum(
        jnp.where(slot_of[None, :] == numbers[:, None], numbers[None, :], 0), axis=1
    )
    starts = jnp.cumsum(image_sizes, axis=1) - image_sizes
    sizes_flat = image_sizes.reshape(-1)
    inner = jnp.arange(most, dtype=jnp.int32)
    groups = jnp.arange(n_row, dtype=jnp.int32)
    my_dest = lax.dynamic_slice_in_dim(slot_of, row_index * IMG_ROW, IMG_ROW) // IMG_ROW
    my_starts = lax.dynamic_index_in_dim(starts, row_index, 0, keepdims=False)
    match = my_dest[None, :] == groups[:, None]
    start_to = jnp.sum(jnp.where(match, my_starts[None, :], 0), axis=1)
    padded = jnp.concatenate([projected, jnp.zeros((most, out_dev), projected.dtype)], axis=0)
    rows = jnp.clip(start_to[:, None] + inner[None, :], 0, padded.shape[0] - 1)
    send = jnp.take(padded, rows.reshape(-1), axis=0).reshape(n_row, most, out_dev)
    recv = lax.all_to_all(send, "row", 0, 0, tiled=True)

    request = lax.dynamic_slice_in_dim(req_at_slot, row_index * IMG_ROW, IMG_ROW)
    source = request // IMG_ROW
    taken = jnp.take(recv, source, axis=0)
    valid = inner[None, :] < sizes_flat[request][:, None]
    blocks = jnp.where(valid[:, :, None], taken, jnp.zeros_like(taken)).astype(jnp.float32)
    squares = jnp.sum(blocks * blocks, axis=(1, 2))
    peaks = jnp.max(jnp.abs(blocks), axis=(1, 2))
    stats = lax.all_gather(jnp.concatenate([squares, peaks]), "col", axis=0, tiled=False)
    squares = jnp.sum(stats[:, :IMG_ROW], axis=0)
    peaks = jnp.max(stats[:, IMG_ROW:], axis=0)
    slot_size = sizes_flat[request].astype(jnp.float32)
    req_norm = jnp.sqrt(squares / (slot_size * OUT) + 1e-06)
    merged_out = (
        (blocks / req_norm[:, None, None]).astype(jnp.bfloat16).reshape(IMG_ROW * most, out_dev)
    )
    return (merged_out, req_norm, peaks)


def solution(mesh):
    in_specs = (
        P(("row", "col"), None),
        P(),
        P(),
        P(),
        P(),
        P(None, "row", "col"),
        P(None, "col", "row"),
        P(None, "row", "col"),
        P(None, "col", "row"),
        P(),
        P(),
        P("row", "col"),
    )
    out_specs = (P("row", "col"), P("row"), P("row"))
    return jax.shard_map(local, mesh=mesh, in_specs=in_specs, out_specs=out_specs, check_vma=False)
```

```python
import jax
import jax.numpy as jnp
from jax import lax
from jax.sharding import PartitionSpec as P


D = 1280
HEAD_DIM = 80
OUT = 4096
IMG_ROW = 8


def layer_norm(values, gain, bias):
    center = jnp.mean(values, axis=-1, keepdims=True)
    shifted = values - center
    spread = jnp.mean(shifted * shifted, axis=-1, keepdims=True)
    return shifted * lax.rsqrt(spread + 1e-06) * gain + bias


def segment_ids(sizes_row, count):
    bounds = jnp.cumsum(sizes_row)
    merged_index = jnp.arange(count, dtype=jnp.int32) // 4
    return jnp.sum((merged_index[:, None] >= bounds[None, :]).astype(jnp.int32), axis=1)


def attend(qkv, segments):
    count = qkv.shape[0]
    width = min(512, count)
    query = qkv[:, :, 0]
    keys = qkv[:, :, 1]
    values = qkv[:, :, 2]
    results = []
    for offset in range(0, count, width):
        scores = jnp.einsum(
            "qhd,khd->hqk", query[offset : offset + width], keys, preferred_element_type=jnp.float32
        ) * HEAD_DIM ** (-0.5)
        same = segments[offset : offset + width, None] == segments[None, :]
        scores = jnp.where(same[None], scores, -1e30)
        peak = jnp.max(scores, axis=-1, keepdims=True)
        expo = jnp.exp(scores - peak)
        weights = (expo / jnp.sum(expo, axis=-1, keepdims=True)).astype(jnp.bfloat16)
        context = jnp.einsum("hqk,khd->qhd", weights, values, preferred_element_type=jnp.float32)
        results.append(context.astype(jnp.bfloat16).reshape(width, -1))
    return jnp.concatenate(results, axis=0)


def row_gather(block):
    n_row = lax.axis_size("row")
    send = jnp.broadcast_to(block[None], (n_row,) + block.shape)
    received = lax.all_to_all(send, "row", 0, 0, tiled=True)
    return received.reshape((n_row * block.shape[0],) + block.shape[1:])


def local(
    tokens,
    image_sizes,
    slot_of,
    ln_gain,
    ln_bias,
    w_qkv,
    w_out,
    w_up,
    w_down,
    merge_gain,
    merge_bias,
    w_merge,
):
    n_col = lax.axis_size("col")
    n_row = lax.axis_size("row")
    row_index = lax.axis_index("row")
    tok_dev = tokens.shape[0]
    tok_row = tok_dev * n_col
    merged_row = tok_row // 4
    most = merged_row * 3 // 16
    sizes_here = lax.dynamic_index_in_dim(image_sizes, row_index, 0, keepdims=False)
    segments = segment_ids(sizes_here, tok_row)

    qkv_cols = w_qkv.shape[2]
    first = row_gather(jnp.concatenate([w_qkv[0], w_out[0].T], axis=1))
    up_cols = w_up.shape[2]
    second = row_gather(jnp.concatenate([w_up[0], w_down[0].T], axis=1))
    merge_full = row_gather(w_merge)
    qkv_full = first[:, :qkv_cols]
    out_t = first[:, qkv_cols:]
    up_full = second[:, :up_cols]
    down_t = second[:, up_cols:]
    contract_t = (((1,), (1,)), ((), ()))

    stream = tokens
    normed = layer_norm(stream.astype(jnp.float32), ln_gain[0, 0], ln_bias[0, 0]).astype(
        jnp.bfloat16
    )
    normed_all = lax.all_gather(normed, "col", axis=0, tiled=True)
    qkv = jnp.dot(normed_all, qkv_full, preferred_element_type=jnp.float32)
    qkv = qkv.astype(jnp.bfloat16).reshape(tok_row, -1, 3, HEAD_DIM)
    context = attend(qkv, segments)
    head_cols = context.shape[1]
    col_index = lax.axis_index("col")
    out_all = lax.all_gather(out_t.T, "col", axis=0, tiled=True)
    attn_out = jnp.zeros((tok_dev, D), jnp.float32)
    for shift in range(n_col):
        target = (col_index + shift) % n_col
        block = lax.dynamic_slice_in_dim(context, target * tok_dev, tok_dev, 0)
        if shift:
            pairs = [(i, (i + shift) % n_col) for i in range(n_col)]
            block = lax.ppermute(block, "col", pairs)
        source = (col_index - shift) % n_col
        rows = lax.dynamic_slice_in_dim(out_all, source * head_cols, head_cols, 0)
        term = jnp.dot(block, rows, preferred_element_type=jnp.float32)
        attn_out = attn_out + term.astype(jnp.bfloat16).astype(jnp.float32)
    stream = (stream.astype(jnp.float32) + attn_out).astype(jnp.bfloat16)
    normed = layer_norm(stream.astype(jnp.float32), ln_gain[0, 1], ln_bias[0, 1]).astype(
        jnp.bfloat16
    )
    normed_mlp = lax.all_gather(normed, "col", axis=0, tiled=True)
    up_value = jnp.dot(normed_mlp, up_full, preferred_element_type=jnp.float32)
    hidden = jax.nn.gelu(up_value, approximate=False).astype(jnp.bfloat16)
    mlp_terms = lax.dot_general(
        hidden, down_t, contract_t, preferred_element_type=jnp.float32
    )
    mlp_terms = mlp_terms.astype(jnp.bfloat16)
    mlp_out = jnp.zeros((tok_dev, D), jnp.float32)
    for shift in range(n_col):
        target = (col_index + shift) % n_col
        block = lax.dynamic_slice_in_dim(mlp_terms, target * tok_dev, tok_dev, 0)
        if shift:
            pairs = [(i, (i + shift) % n_col) for i in range(n_col)]
            block = lax.ppermute(block, "col", pairs)
        mlp_out = mlp_out + block.astype(jnp.float32)
    stream = (stream.astype(jnp.float32) + mlp_out).astype(jnp.bfloat16)
    merged = layer_norm(stream.astype(jnp.float32), merge_gain, merge_bias).astype(jnp.bfloat16)
    merged = merged.reshape(tok_dev // 4, 4 * D)
    merged_all = lax.all_gather(merged, "col", axis=0, tiled=True)
    out_dev = w_merge.shape[1]
    projected = jnp.dot(merged_all, merge_full, preferred_element_type=jnp.float32).astype(
        jnp.bfloat16
    )

    reqs = slot_of.shape[0]
    numbers = jnp.arange(reqs, dtype=jnp.int32)
    req_at_slot = jnp.sum(
        jnp.where(slot_of[None, :] == numbers[:, None], numbers[None, :], 0), axis=1
    )
    starts = jnp.cumsum(image_sizes, axis=1) - image_sizes
    sizes_flat = image_sizes.reshape(-1)
    inner = jnp.arange(most, dtype=jnp.int32)
    groups = jnp.arange(n_row, dtype=jnp.int32)
    my_dest = lax.dynamic_slice_in_dim(slot_of, row_index * IMG_ROW, IMG_ROW) // IMG_ROW
    my_starts = lax.dynamic_index_in_dim(starts, row_index, 0, keepdims=False)
    match = my_dest[None, :] == groups[:, None]
    start_to = jnp.sum(jnp.where(match, my_starts[None, :], 0), axis=1)
    padded = jnp.concatenate([projected, jnp.zeros((most, out_dev), projected.dtype)], axis=0)
    rows = jnp.clip(start_to[:, None] + inner[None, :], 0, padded.shape[0] - 1)
    send = jnp.take(padded, rows.reshape(-1), axis=0).reshape(n_row, most, out_dev)
    recv = lax.all_to_all(send, "row", 0, 0, tiled=True)

    request = lax.dynamic_slice_in_dim(req_at_slot, row_index * IMG_ROW, IMG_ROW)
    source = request // IMG_ROW
    taken = jnp.take(recv, source, axis=0)
    valid = inner[None, :] < sizes_flat[request][:, None]
    blocks = jnp.where(valid[:, :, None], taken, jnp.zeros_like(taken)).astype(jnp.float32)
    squares = jnp.sum(blocks * blocks, axis=(1, 2))
    peaks = jnp.max(jnp.abs(blocks), axis=(1, 2))
    mine = jnp.concatenate([squares, peaks])
    shares = [mine]
    for shift in range(1, n_col):
        pairs = [(i, (i + shift) % n_col) for i in range(n_col)]
        shares.append(lax.ppermute(mine, "col", pairs))
    by_shift = jnp.stack(shares)
    order = (col_index - jnp.arange(n_col, dtype=jnp.int32)) % n_col
    stats = jnp.take(by_shift, order, axis=0)
    squares = jnp.sum(stats[:, :IMG_ROW], axis=0)
    peaks = jnp.max(stats[:, IMG_ROW:], axis=0)
    slot_size = sizes_flat[request].astype(jnp.float32)
    req_norm = jnp.sqrt(squares / (slot_size * OUT) + 1e-06)
    merged_out = (
        (blocks / req_norm[:, None, None]).astype(jnp.bfloat16).reshape(IMG_ROW * most, out_dev)
    )
    return (merged_out, req_norm, peaks)


def solution(mesh):
    in_specs = (
        P(("row", "col"), None),
        P(),
        P(),
        P(),
        P(),
        P(None, "row", "col"),
        P(None, "col", "row"),
        P(None, "row", "col"),
        P(None, "col", "row"),
        P(),
        P(),
        P("row", "col"),
    )
    out_specs = (P("row", "col"), P("row"), P("row"))
    return jax.shard_map(local, mesh=mesh, in_specs=in_specs, out_specs=out_specs, check_vma=False)
```

```python
import jax
import jax.numpy as jnp
from jax import lax
from jax.sharding import PartitionSpec as P


D = 1280
HEAD_DIM = 80
OUT = 4096
IMG_ROW = 8


def layer_norm(values, gain, bias):
    center = jnp.mean(values, axis=-1, keepdims=True)
    shifted = values - center
    spread = jnp.mean(shifted * shifted, axis=-1, keepdims=True)
    return shifted * lax.rsqrt(spread + 1e-06) * gain + bias


def segment_ids(sizes_row, count):
    bounds = jnp.cumsum(sizes_row)
    merged_index = jnp.arange(count, dtype=jnp.int32) // 4
    return jnp.sum((merged_index[:, None] >= bounds[None, :]).astype(jnp.int32), axis=1)


def attend(qkv, segments):
    count = qkv.shape[0]
    width = min(512, count)
    query = qkv[:, :, 0]
    keys = qkv[:, :, 1]
    values = qkv[:, :, 2]
    results = []
    for offset in range(0, count, width):
        scores = jnp.einsum(
            "qhd,khd->hqk", query[offset : offset + width], keys, preferred_element_type=jnp.float32
        ) * HEAD_DIM ** (-0.5)
        same = segments[offset : offset + width, None] == segments[None, :]
        scores = jnp.where(same[None], scores, -1e30)
        peak = jnp.max(scores, axis=-1, keepdims=True)
        expo = jnp.exp(scores - peak)
        weights = (expo / jnp.sum(expo, axis=-1, keepdims=True)).astype(jnp.bfloat16)
        context = jnp.einsum("hqk,khd->qhd", weights, values, preferred_element_type=jnp.float32)
        results.append(context.astype(jnp.bfloat16).reshape(width, -1))
    return jnp.concatenate(results, axis=0)


def row_gather(block):
    n_row = lax.axis_size("row")
    send = jnp.broadcast_to(block[None], (n_row,) + block.shape)
    received = lax.all_to_all(send, "row", 0, 0, tiled=True)
    return received.reshape((n_row * block.shape[0],) + block.shape[1:])


def local(
    tokens,
    image_sizes,
    slot_of,
    ln_gain,
    ln_bias,
    w_qkv,
    w_out,
    w_up,
    w_down,
    merge_gain,
    merge_bias,
    w_merge,
):
    n_col = lax.axis_size("col")
    n_row = lax.axis_size("row")
    row_index = lax.axis_index("row")
    tok_dev = tokens.shape[0]
    tok_row = tok_dev * n_col
    merged_row = tok_row // 4
    most = merged_row * 3 // 16
    sizes_here = lax.dynamic_index_in_dim(image_sizes, row_index, 0, keepdims=False)
    segments = segment_ids(sizes_here, tok_row)

    qkv_cols = w_qkv.shape[2]
    first = row_gather(jnp.concatenate([w_qkv[0], w_out[0].T], axis=1))
    up_cols = w_up.shape[2]
    second = row_gather(jnp.concatenate([w_up[0], w_down[0].T], axis=1))
    merge_full = row_gather(w_merge)
    qkv_full = first[:, :qkv_cols]
    out_t = first[:, qkv_cols:]
    up_full = second[:, :up_cols]
    down_t = second[:, up_cols:]
    contract_t = (((1,), (1,)), ((), ()))

    stream = tokens
    normed = layer_norm(stream.astype(jnp.float32), ln_gain[0, 0], ln_bias[0, 0]).astype(
        jnp.bfloat16
    )
    normed_all = lax.all_gather(normed, "col", axis=0, tiled=True)
    qkv = jnp.dot(normed_all, qkv_full, preferred_element_type=jnp.float32)
    qkv = qkv.astype(jnp.bfloat16).reshape(tok_row, -1, 3, HEAD_DIM)
    context = attend(qkv, segments)
    head_cols = context.shape[1]
    col_index = lax.axis_index("col")
    out_all = lax.all_gather(out_t.T, "col", axis=0, tiled=True)
    attn_out = jnp.zeros((tok_dev, D), jnp.float32)
    for shift in range(n_col):
        target = (col_index + shift) % n_col
        block = lax.dynamic_slice_in_dim(context, target * tok_dev, tok_dev, 0)
        if shift:
            pairs = [(i, (i + shift) % n_col) for i in range(n_col)]
            block = lax.ppermute(block, "col", pairs)
        source = (col_index - shift) % n_col
        rows = lax.dynamic_slice_in_dim(out_all, source * head_cols, head_cols, 0)
        term = jnp.dot(block, rows, preferred_element_type=jnp.float32)
        attn_out = attn_out + term.astype(jnp.bfloat16).astype(jnp.float32)
    stream = (stream.astype(jnp.float32) + attn_out).astype(jnp.bfloat16)
    normed = layer_norm(stream.astype(jnp.float32), ln_gain[0, 1], ln_bias[0, 1]).astype(
        jnp.bfloat16
    )
    normed_mlp = lax.all_gather(normed, "col", axis=0, tiled=True)
    up_value = jnp.dot(normed_mlp, up_full, preferred_element_type=jnp.float32)
    hidden = jax.nn.gelu(up_value, approximate=False).astype(jnp.bfloat16)
    mlp_terms = lax.dot_general(
        hidden, down_t, contract_t, preferred_element_type=jnp.float32
    )
    mlp_terms = mlp_terms.astype(jnp.bfloat16)
    mlp_out = jnp.zeros((tok_dev, D), jnp.float32)
    for shift in range(n_col):
        target = (col_index + shift) % n_col
        block = lax.dynamic_slice_in_dim(mlp_terms, target * tok_dev, tok_dev, 0)
        if shift:
            pairs = [(i, (i + shift) % n_col) for i in range(n_col)]
            block = lax.ppermute(block, "col", pairs)
        mlp_out = mlp_out + block.astype(jnp.float32)
    stream = (stream.astype(jnp.float32) + mlp_out).astype(jnp.bfloat16)
    merged = layer_norm(stream.astype(jnp.float32), merge_gain, merge_bias).astype(jnp.bfloat16)
    merged = merged.reshape(tok_dev // 4, 4 * D)
    gathered = [merged]
    for shift in range(1, n_col):
        pairs = [(i, (i + shift) % n_col) for i in range(n_col)]
        gathered.append(lax.ppermute(merged, "col", pairs))
    merged_order = (col_index - jnp.arange(n_col, dtype=jnp.int32)) % n_col
    merged_all = jnp.take(jnp.stack(gathered), merged_order, axis=0).reshape(-1, merged.shape[1])
    out_dev = w_merge.shape[1]
    projected = jnp.dot(merged_all, merge_full, preferred_element_type=jnp.float32).astype(
        jnp.bfloat16
    )

    reqs = slot_of.shape[0]
    numbers = jnp.arange(reqs, dtype=jnp.int32)
    req_at_slot = jnp.sum(
        jnp.where(slot_of[None, :] == numbers[:, None], numbers[None, :], 0), axis=1
    )
    starts = jnp.cumsum(image_sizes, axis=1) - image_sizes
    sizes_flat = image_sizes.reshape(-1)
    inner = jnp.arange(most, dtype=jnp.int32)
    groups = jnp.arange(n_row, dtype=jnp.int32)
    my_dest = lax.dynamic_slice_in_dim(slot_of, row_index * IMG_ROW, IMG_ROW) // IMG_ROW
    my_starts = lax.dynamic_index_in_dim(starts, row_index, 0, keepdims=False)
    match = my_dest[None, :] == groups[:, None]
    start_to = jnp.sum(jnp.where(match, my_starts[None, :], 0), axis=1)
    padded = jnp.concatenate([projected, jnp.zeros((most, out_dev), projected.dtype)], axis=0)
    rows = jnp.clip(start_to[:, None] + inner[None, :], 0, padded.shape[0] - 1)
    send = jnp.take(padded, rows.reshape(-1), axis=0).reshape(n_row, most, out_dev)
    recv = lax.all_to_all(send, "row", 0, 0, tiled=True)

    request = lax.dynamic_slice_in_dim(req_at_slot, row_index * IMG_ROW, IMG_ROW)
    source = request // IMG_ROW
    taken = jnp.take(recv, source, axis=0)
    valid = inner[None, :] < sizes_flat[request][:, None]
    blocks = jnp.where(valid[:, :, None], taken, jnp.zeros_like(taken)).astype(jnp.float32)
    squares = jnp.sum(blocks * blocks, axis=(1, 2))
    peaks = jnp.max(jnp.abs(blocks), axis=(1, 2))
    mine = jnp.concatenate([squares, peaks])
    shares = [mine]
    for shift in range(1, n_col):
        pairs = [(i, (i + shift) % n_col) for i in range(n_col)]
        shares.append(lax.ppermute(mine, "col", pairs))
    by_shift = jnp.stack(shares)
    order = (col_index - jnp.arange(n_col, dtype=jnp.int32)) % n_col
    stats = jnp.take(by_shift, order, axis=0)
    squares = jnp.sum(stats[:, :IMG_ROW], axis=0)
    peaks = jnp.max(stats[:, IMG_ROW:], axis=0)
    slot_size = sizes_flat[request].astype(jnp.float32)
    req_norm = jnp.sqrt(squares / (slot_size * OUT) + 1e-06)
    merged_out = (
        (blocks / req_norm[:, None, None]).astype(jnp.bfloat16).reshape(IMG_ROW * most, out_dev)
    )
    return (merged_out, req_norm, peaks)


def solution(mesh):
    in_specs = (
        P(("row", "col"), None),
        P(),
        P(),
        P(),
        P(),
        P(None, "row", "col"),
        P(None, "col", "row"),
        P(None, "row", "col"),
        P(None, "col", "row"),
        P(),
        P(),
        P("row", "col"),
    )
    out_specs = (P("row", "col"), P("row"), P("row"))
    return jax.shard_map(local, mesh=mesh, in_specs=in_specs, out_specs=out_specs, check_vma=False)
```
